512 devices in a mesh: slab: 8 (over z_hi, core), vel: 64 (over x, y, z_lo).
Axes of the slice: x: 4, y: 4, z: 16 (z_hi: 4, z_lo: 4; z = z_hi * 4 + z_lo), core: 2. Of those that a mesh axis runs over, the one named last changes fastest.
Arguments:
- f_start: float32 [4096, 8, 8, 128], P('vel', 'slab'), as said below
- links: int32 [3, 8, 8, 128], P(None, 'slab'), may hold values 0 or 1
- solid: int32 [8, 8, 128], P('slab'), may hold values 0 or 1
Outputs:
- f_final: float32 [4096, 8, 8, 128], P('vel', 'slab')
The draws below stay inside these ranges and needn't reach their ends.
Inputs may be any that keep to these rules, and one draw needn't show every extreme that they name: `f_start`: every entry is positive.
All inputs are finite; a program needn't handle non-finite values. No bound on the sum of `links` or of `solid` on one device may be relied on, other than what follows from the above.
Results may differ from the reference program's by a relative error of at most 0.0003.
Values sent between devices are 32-bit elements; how exact they have to be, the bound alone decides.
No kernel may reach another device: no remote copies, remote signals or barrier semaphores. Data moves between devices by JAX's collectives and lax.ppermute only.
A program may use at most 64 MiB of HBM per device.

```python
import math
import jax
import jax.numpy as jnp
from jax import lax

NQ = 16
NY = 8
NZ = 128
STEPS = 2
SWEEPS = 2
NX = 8


def draw_f_start(key, part):
    keys = jax.random.split(jax.random.fold_in(key, 17), 4)
    total_vel = NQ ** 3
    grid = (NX, NY, NZ)
    matter_per_volume = jax.random.uniform(keys[0], grid, jnp.float32, 0.5, 2.0)
    factor = jax.random.uniform(keys[3], (total_vel,) + grid, jnp.float32, 0.5, 1.5)
    drift = jax.random.uniform(keys[1], (3,) + grid, jnp.float32, -0.5, 0.5)
    warmth = jax.random.uniform(keys[2], grid, jnp.float32, 0.6, 1.5)
    index = jnp.arange(total_vel).astype(jnp.int32)
    comps = jnp.stack([index % NQ, index // NQ % NQ, index // (NQ * NQ)]).astype(jnp.float32)
    lattice = (comps - (NQ - 1) / 2.0) * 0.6
    spread = jnp.zeros((total_vel,) + grid, jnp.float32)
    for axis_dim in range(3):
        offset = lattice[axis_dim][:, None, None, None] - drift[axis_dim][None]
        spread = spread + offset * offset
    return matter_per_volume * warmth ** (-1.5) * jnp.exp(-spread / (2.0 * warmth)) * factor


def place_ends(array, own_key, low, largest):
    shape = array.shape
    place = [jax.random.randint(jax.random.fold_in(own_key, axis), (), 0, shape[axis]) for axis in range(len(shape))]
    array = array.at[tuple(place)].set(low)
    longest = shape.index(max(shape))
    place[longest] = (place[longest] + 1) % shape[longest]
    return array.at[tuple(place)].set(largest)


def setup_inputs(seed: int = 0) -> dict:
    arg_keys = jax.random.split(jax.random.key(seed), 4)
    return {
        "f_start": draw_f_start(jax.random.fold_in(arg_keys[3], 71), 0),
        "links": place_ends((jax.random.randint(arg_keys[1], (3, NX, NY, NZ), 0, 4) < 3).astype(jnp.int32), jax.random.fold_in(arg_keys[1], 1), 0, 1),
        "solid": place_ends((jax.random.randint(arg_keys[2], (NX, NY, NZ), 0, 8) < 1).astype(jnp.int32), jax.random.fold_in(arg_keys[2], 1), 0, 1),
    }


SPACING = 0.6
COUPLING = 1.0
COURANT = 0.06
RELAXATION_FREQ = 0.5
VISCOUS_TO_HEAT = 2.0 / 3.0
QUAD_WEIGHT = SPACING ** 3 / (2.0 * math.pi) ** 1.5


def lattice_of(first, number):
    index = (first + jnp.arange(number)).astype(jnp.int32)
    comp_x = index % NQ
    comp_y = (index // NQ) % NQ
    comp_z = index // (NQ * NQ)
    stacked = jnp.stack([comp_x, comp_y, comp_z]).astype(jnp.float32)
    return (stacked - (NQ - 1) / 2.0) * SPACING


def moment_basis(lattice):
    overall_work_content = 0.5 * jnp.sum(lattice * lattice, axis=0)
    rows = [jnp.ones_like(overall_work_content), lattice[0], lattice[1], lattice[2], overall_work_content,
            lattice[0] * overall_work_content, lattice[1] * overall_work_content, lattice[2] * overall_work_content]
    return jnp.stack(rows) * QUAD_WEIGHT


def shift_down(values, axis_dim):
    pads = [(0, 0)] * values.ndim
    pads[axis_dim] = (1, 0)
    return lax.slice_in_dim(jnp.pad(values, pads), 0, values.shape[axis_dim], axis=axis_dim)


def shift_up(values, axis_dim):
    pads = [(0, 0)] * values.ndim
    pads[axis_dim] = (0, 1)
    return lax.slice_in_dim(jnp.pad(values, pads), 1, values.shape[axis_dim] + 1, axis=axis_dim)


def macro_state(predicted):
    matter_per_volume = predicted[0]
    mean_flow_vector = predicted[1:4] / matter_per_volume
    overall_work_content = predicted[4]
    fluid_hotness_level = (2.0 * overall_work_content / matter_per_volume - jnp.sum(mean_flow_vector * mean_flow_vector, axis=0)) / 3.0
    fluid_normal_stress = matter_per_volume * fluid_hotness_level
    heat_current_vector = predicted[5:8] - mean_flow_vector * (overall_work_content + fluid_normal_stress)
    relaxation_update = RELAXATION_FREQ * matter_per_volume * fluid_hotness_level ** 0.28
    profile_multiplier = (1.0 - VISCOUS_TO_HEAT) * heat_current_vector / (5.0 * fluid_normal_stress * fluid_hotness_level)
    perturbation_height = matter_per_volume * fluid_hotness_level ** -1.5
    return mean_flow_vector, fluid_hotness_level, relaxation_update, profile_multiplier, perturbation_height


def upwind_local(dist, speed, axis_dim):
    return jnp.where(speed > 0, shift_down(dist, axis_dim), shift_up(dist, axis_dim))


def transport(dist, upwind_x, lattice, particle_population, open_up, open_low, solid):
    mean_flow_vector, fluid_hotness_level, relaxation_update, profile_multiplier, perturbation_height = particle_population
    peculiar = lattice[:, :, None, None, None] - mean_flow_vector[:, None]
    acoustic_celerity_power = jnp.sum(peculiar * peculiar, axis=0)
    matching_arrangement = jnp.sum(peculiar * profile_multiplier[:, None], axis=0)
    relaxed_distribution_goal = perturbation_height * jnp.exp(-acoustic_celerity_power / (2.0 * fluid_hotness_level)) * (1.0 + matching_arrangement * (acoustic_celerity_power / fluid_hotness_level - 5.0))
    flux = jnp.zeros_like(dist)
    for axis_dim in range(3):
        speed = lattice[axis_dim][:, None, None, None]
        rising = speed > 0
        outward = jnp.where(rising, open_up[axis_dim], open_low[axis_dim])
        inward = jnp.where(rising, open_low[axis_dim], open_up[axis_dim])
        if axis_dim == 0:
            neighbour = upwind_x
        else:
            neighbour = upwind_local(dist, speed, axis_dim + 1)
        flux = flux + jnp.abs(speed) * (outward * dist - inward * neighbour)
    fresh = (dist - COURANT * flux + relaxation_update * relaxed_distribution_goal) / (1.0 + relaxation_update)
    return jnp.where(solid > 0, dist, fresh)


def reference(f_start, links, solid):
    total_vel = NQ ** 3
    open_up = links.astype(jnp.float32)
    open_low = jnp.stack([shift_down(open_up[0], 0), shift_down(open_up[1], 1), shift_down(open_up[2], 2)])
    count = jnp.sum(open_up, axis=0) + jnp.sum(open_low, axis=0)
    lattice = lattice_of(0, total_vel)
    basis = moment_basis(lattice)
    block_rows = 256
    blocks = total_vel // block_rows
    lattice_blocks = jnp.transpose(lattice.reshape(3, blocks, block_rows), (1, 0, 2))
    dist = f_start
    for repeat in range(STEPS):
        moments = jnp.dot(basis, dist.reshape(total_vel, -1), precision=lax.Precision.HIGHEST)
        moments = moments.reshape((8,) + dist.shape[1:])
        predicted = moments
        for sweeping in range(SWEEPS):
            beside_all = (shift_up(predicted, 1) * open_up[0] + shift_down(predicted, 1) * open_low[0]
                      + shift_up(predicted, 2) * open_up[1] + shift_down(predicted, 2) * open_low[1]
                      + shift_up(predicted, 3) * open_up[2] + shift_down(predicted, 3) * open_low[2])
            predicted = (moments + COUPLING * beside_all) / (1.0 + COUPLING * count)
        particle_population = macro_state(predicted)

        def advance(pair):
            piece, part_lattice = pair
            speed = part_lattice[0][:, None, None, None]
            upwind_x = upwind_local(piece, speed, 1)
            return transport(piece, upwind_x, part_lattice, particle_population, open_up, open_low, solid)

        stacked = dist.reshape((blocks, block_rows) + dist.shape[1:])
        dist = lax.map(advance, (stacked, lattice_blocks)).reshape(dist.shape)
    return dist
```

```python
import math

import jax
import jax.numpy as jnp
from jax import lax
from jax.experimental import pallas as pl
from jax.experimental.pallas import tpu as pltpu
from jax.sharding import Mesh
from jax.sharding import PartitionSpec as P

NQ = 16
HALF = NQ // 2
LY = 4
NS = 8
NY, NZ = 8, 128
SPACING = 0.6
COURANT = 0.06
RELAXATION_FREQ = 0.5
VISCOUS_TO_HEAT = 2.0 / 3.0
QUAD_WEIGHT = SPACING**3 / (2.0 * math.pi) ** 1.5
F32 = jnp.float32

SLAB = ("zh", "core")
VEL = ("x", "y", "zl")


def rows_and_lanes():
    row = lax.broadcasted_iota(jnp.int32, (NY, NZ), 0)
    lane = lax.broadcasted_iota(jnp.int32, (NY, NZ), 1)
    return row, lane


def down(v, axis):
    return pltpu.roll(v, 1, axis)


def up(v, axis):
    return pltpu.roll(v, v.shape[axis] - 1, axis)


def speed_of(index):
    return (index.astype(F32) - (NQ - 1) / 2.0) * SPACING


def sides(links, axis, first, last, rising):
    open_up = links
    open_low = jnp.where(first, 0.0, down(links, axis))
    inner_up = jnp.where(last, 0.0, links)
    return jnp.where(rising, open_up, open_low), jnp.where(rising, open_low, inner_up)


def moments_kernel(place, f_ref, links_ref, out_ref):
    rank = place[0]
    row, lane = rows_and_lanes()
    zv = speed_of(rank // 4)
    z_rising, y_rising = rank // 4 >= HALF, rank % 4 >= 2
    ly = links_ref[1].astype(F32)
    lz = links_ref[2].astype(F32)
    out_y, in_y = sides(ly, 0, row == 0, row == NY - 1, y_rising)
    out_z, in_z = sides(lz, 1, lane == 0, lane == NZ - 1, z_rising)
    shift_y = jnp.where(y_rising, 1, NY - 1)
    shift_z = jnp.where(z_rising, 1, NZ - 1)
    az = COURANT * jnp.abs(zv)
    out_z, in_z = az * out_z, az * in_z
    totals = None
    for jy in range(LY):
        yv = speed_of(rank % 4 * LY + jy)
        ay = COURANT * jnp.abs(yv)
        pos, neg = [None] * 5, [None] * 5
        for j in range(HALF):
            a = (j + 0.5) * SPACING
            fp = f_ref[jy * NQ + HALF + j]
            fn = f_ref[jy * NQ + HALF - 1 - j]
            for n in range(5):
                wp = fp if n == 0 else fp * a**n
                wn = fn if n == 0 else fn * a**n
                pos[n] = wp if pos[n] is None else pos[n] + wp
                neg[n] = wn if neg[n] is None else neg[n] + wn
        full = [pos[n] + neg[n] if n % 2 == 0 else pos[n] - neg[n] for n in range(4)]
        keep = 1.0 - ay * out_y - out_z
        moved = [
            keep * v + (ay * in_y) * pltpu.roll(v, shift_y, 0) + in_z * pltpu.roll(v, shift_z, 1)
            for v in full
        ]
        plus = pos[1:5]
        minus = [neg[1], -neg[2], neg[3], -neg[4]]
        q = yv * yv + zv * zv
        parts = []
        for a0, a1, a2, a3 in (full, moved, plus, minus):
            e0 = 0.5 * (a2 + q * a0)
            e1 = 0.5 * (a3 + q * a1)
            parts.append([a0, a1, yv * a0, e0, e1, yv * e0])
        if totals is None:
            totals = parts
        else:
            totals = [[t + p for t, p in zip(ts, ps)] for ts, ps in zip(totals, parts)]
    for kind, (b0, b1, by, e0, e1, ey) in enumerate(totals):
        for k, v in enumerate((b0, b1, by, zv * b0, e0, e1, ey, zv * e0)):
            out_ref[pl.ds(k * 32 + kind, NY, stride=4), :] = v * QUAD_WEIGHT


def owner_kernel(place, parts_ref, links_ref, solid_ref, out_ref):
    rank = place[0]
    k, y = rank // 8, rank % 8
    total = parts_ref[0]
    for i in range(1, 32):
        total = total + parts_ref[i]
    total = total + pltpu.roll(total, 4, 0)
    row = lax.broadcasted_iota(jnp.int32, (8, NZ), 0)
    flags = [links_ref[a, pl.ds(y, 1), :].astype(F32) for a in range(3)]
    flags.append(solid_ref[pl.ds(y, 1), :].astype(F32))
    kind = k % 4
    own = jnp.where(kind == 0, flags[0], jnp.where(kind == 1, flags[1], jnp.where(kind == 2, flags[2], flags[3])))
    block = jnp.where(row < 4, total, jnp.where(row == 4, flags[0], jnp.where(row == 5, own, 0.0)))
    for i in range(out_ref.shape[0]):
        out_ref[i] = block


def combine_kernel(place, parts_ref, out_ref):
    rank = place[0]
    kinds = [parts_ref[pl.ds(kind, 32, stride=8), :] for kind in range(6)]
    m0, q, hp, hm, lx, own = kinds
    row = lax.broadcasted_iota(jnp.int32, (32, NZ), 0)
    low = jnp.where(row < 4, 0.0, pltpu.roll(lx, 4, 0))
    inner = jnp.where(row >= 28, 0.0, lx)
    mt = q - COURANT * (lx * hp + low * hm - low * pltpu.roll(hp, 4, 0) - inner * pltpu.roll(hm, 28, 0))
    half = jnp.where(rank // 32 == 0, own[:16], own[16:])
    for i in range(out_ref.shape[0]):
        out_ref[i, 0:32, :] = m0
        out_ref[i, 32:64, :] = mt
        out_ref[i, 64:80, :] = half


def macro_state(p):
    rho = p[0]
    inv = 1.0 / rho
    u = [p[1 + a] * inv for a in range(3)]
    energy = p[4]
    u2 = u[0] * u[0] + u[1] * u[1] + u[2] * u[2]
    temp = (2.0 * energy * inv - u2) / 3.0
    stress = rho * temp
    nu = RELAXATION_FREQ * rho * jnp.exp(0.28 * jnp.log(temp))
    scale = (1.0 - VISCOUS_TO_HEAT) / (5.0 * stress * temp)
    s = [(p[5 + a] - u[a] * (energy + stress)) * scale for a in range(3)]
    inv_t = 1.0 / temp
    height = rho * inv_t * lax.sqrt(inv_t)
    return u, u2, inv_t, nu, s, height


def xi(i):
    return (i - (NQ - 1) / 2.0) * SPACING


def target_moments(u, u2, inv_t, s, height):
    half_t = -0.5 * inv_t
    one_d = []
    for a in range(3):
        m = [None] * 7
        for i in range(NQ):
            c = xi(i) - u[a]
            t = jnp.exp(c * c * half_t)
            for n in range(7):
                m[n] = t if m[n] is None else m[n] + t
                if n < 6:
                    t = t * c
        one_d.append(m)
    x, y, z = one_d
    s5 = [-5.0 * v for v in s]
    st = [v * inv_t for v in s]
    cache = {}

    def xy(i, j):
        if (i, j) not in cache:
            cache[i, j] = x[i] * y[j]
        return cache[i, j]

    def plain(i, j, k):
        return xy(i, j) * z[k]

    def mean(i, j, k):
        total = plain(i, j, k)
        for a in range(3):
            e = [i, j, k]
            e[a] += 1
            square = None
            for b in range(3):
                d = list(e)
                d[b] += 2
                t = plain(*d)
                square = t if square is None else square + t
            total = total + s5[a] * plain(*e) + st[a] * square
        return total

    def unit(*axes):
        e = [0, 0, 0]
        for a in axes:
            e[a] += 1
        return mean(*e)

    n0 = unit()
    n1 = [unit(a) for a in range(3)]
    n2 = {(a, b): unit(a, b) for a in range(3) for b in range(a, 3)}
    n3 = [unit(a, 0, 0) + unit(a, 1, 1) + unit(a, 2, 2) for a in range(3)]
    weight = QUAD_WEIGHT * height
    j_e = 0.5 * (n2[0, 0] + n2[1, 1] + n2[2, 2] + u2 * n0) + u[0] * n1[0] + u[1] * n1[1] + u[2] * n1[2]
    rows = [n0] + [n1[a] + u[a] * n0 for a in range(3)] + [j_e]
    for a in range(3):
        cross = sum(u[b] * n2[min(a, b), max(a, b)] for b in range(3))
        rows.append(0.5 * (n3[a] + u2 * n1[a]) + cross + u[a] * j_e)
    return [weight * r for r in rows]


def neighbours(v, w):
    return w[2] * up(v, 0) + w[3] * down(v, 0) + w[4] * up(v, 1) + w[5] * down(v, 1)


def finish_kernel(
    place, got_ref, f_ref, p1_ref, p2_ref, n1_ref, n2_ref, out_ref, m_ref, l_ref, w_ref, pred_ref, next_ref,
    xe_ref, xc_ref, f1_ref, h1_ref,
):
    rank, slab = place[0], place[1]
    row, lane = rows_and_lanes()
    low_half = row < 4
    zero = jnp.zeros((NY, NZ), F32)

    for a in range(4):
        l_ref[a, 0] = zero
        l_ref[a, NS + 1] = zero

    @pl.loop(0, 8)
    def _(k):
        for t in range(10):
            t0, t1 = got_ref[2 * k, t], got_ref[2 * k + 1, t]
            first = jnp.where(low_half, t0, pltpu.roll(t1, 4, 0))
            second = jnp.where(low_half, pltpu.roll(t0, 4, 0), t1)
            if t < 8:
                m_ref[t // 4, k, 2 * (t % 4)] = first
                m_ref[t // 4, k, 2 * (t % 4) + 1] = second
            else:
                base = 1 + k // 4 * 4 + 2 * (t - 8)
                l_ref[k % 4, base] = first
                l_ref[k % 4, base + 1] = second

    for a in range(7):
        w_ref[a, 0] = zero
        w_ref[a, NS + 1] = zero
    for s in range(NS):
        lx, lx_low = l_ref[0, s + 1], l_ref[0, s]
        ly, lz = l_ref[1, s + 1], l_ref[2, s + 1]
        ly_low = jnp.where(row == 0, 0.0, down(ly, 0))
        lz_low = jnp.where(lane == 0, 0.0, down(lz, 1))
        share = 1.0 / (1.0 + (lx + ly + lz + lx_low + ly_low + lz_low))
        w_ref[0, s + 1] = share * lx if s < NS - 1 else zero
        w_ref[1, s + 1] = share * lx_low
        w_ref[2, s + 1] = jnp.where(row == NY - 1, 0.0, share * ly)
        w_ref[3, s + 1] = share * ly_low
        w_ref[4, s + 1] = jnp.where(lane == NZ - 1, 0.0, share * lz)
        w_ref[5, s + 1] = share * lz_low
        w_ref[6, s + 1] = share

    @pl.loop(0, 8)
    def _(k):
        start = [m_ref[0, k, s] for s in range(NS)]
        now = start
        for _ in range(2):
            new = []
            for s in range(NS):
                w = [w_ref[a, s + 1] for a in range(7)]
                v = w[6] * start[s] + neighbours(now[s], w)
                if s < NS - 1:
                    v = v + w[0] * now[s + 1]
                if s > 0:
                    v = v + w[1] * now[s - 1]
                new.append(v)
            now = new
        for s in range(NS):
            pred_ref[k, s] = now[s]

    for k in range(8):
        for i in (0, 1, NS + 2, NS + 3):
            next_ref[k, i] = zero

    @pl.loop(jnp.maximum(slab - 2, 0), jnp.minimum(slab + 3, NS))
    def _(w):
        u, u2, inv_t, nu, s, height = macro_state([pred_ref[k, w] for k in range(8)])
        goal = target_moments(u, u2, inv_t, s, height)
        body = l_ref[3, w + 1] > 0
        share = 1.0 / (1.0 + nu)
        for k in range(8):
            fresh = (m_ref[1, k, w] + nu * goal[k]) * share
            next_ref[k, w + 2] = jnp.where(body, m_ref[0, k, w], fresh)

    last = []
    for k in range(8):
        around = [next_ref[k, slab + i] for i in range(5)]
        mids = []
        for i in range(3):
            w = [w_ref[a, slab + i] for a in range(7)]
            mids.append(
                w[6] * around[i + 1] + w[0] * around[i + 2] + w[1] * around[i] + neighbours(around[i + 1], w)
            )
        w = [w_ref[a, slab + 1] for a in range(7)]
        last.append(w[6] * around[2] + w[0] * mids[2] + w[1] * mids[0] + neighbours(mids[1], w))

    zv = speed_of(rank // 4)
    z_rising, y_rising = rank // 4 >= HALF, rank % 4 >= 2
    shift_y = jnp.where(y_rising, 1, NY - 1)
    shift_z = jnp.where(z_rising, 1, NZ - 1)
    az = COURANT * jnp.abs(zv)

    def advance(planes, here, halves, source, beside, sink):
        u, u2, inv_t, nu, s, height = macro_state(planes)
        half_t = -0.5 * inv_t
        for i in range(NQ):
            if i // HALF in halves:
                c = xi(i) - u[0]
                c2 = c * c
                xe_ref[i] = jnp.exp(c2 * half_t)
                xc_ref[i] = c2 * inv_t
        share = 1.0 / (1.0 + nu)
        lx, lx_low = l_ref[0, here + 1], l_ref[0, here]
        lx_in = jnp.where(here < NS - 1, lx, 0.0)
        body = l_ref[3, here + 1] > 0
        out_y, in_y = sides(l_ref[1, here + 1], 0, row == 0, row == NY - 1, y_rising)
        out_z, in_z = sides(l_ref[2, here + 1], 1, lane == 0, lane == NZ - 1, z_rising)
        move = COURANT * share
        in_z = az * share * in_z
        cz = zv - u[2]
        out_x = (move * lx_low, move * lx)
        in_x = (move * lx_in, move * lx_low)

        @pl.loop(0, LY)
        def _(jy):
            yv = speed_of(rank % 4 * LY + jy)
            ay = COURANT * jnp.abs(yv)
            cy = yv - u[1]
            c2 = cy * cy + cz * cz
            top = nu * share * height * jnp.exp(c2 * half_t)
            tilt = cy * s[1] + cz * s[2] - u[0] * s[0]
            lift = c2 * inv_t - 5.0
            keep = share * (1.0 - ay * out_y - az * out_z)
            from_y = ay * share * in_y
            for i in range(NQ):
                side = i // HALF
                if side in halves:
                    f = source(jy, i)
                    a = abs(xi(i))
                    goal = top * xe_ref[i] * (1.0 + (xi(i) * s[0] + tilt) * (xc_ref[i] + lift))
                    fresh = f * (keep - a * out_x[side]) + (a * in_x[side]) * beside(jy, i)
                    fresh = fresh + from_y * pltpu.roll(f, shift_y, 0) + in_z * pltpu.roll(f, shift_z, 1)
                    sink[jy * NQ + i] = jnp.where(body, f, fresh + goal)

    def half_of(neg_ref, pos_ref):
        return lambda jy, i: (pos_ref if i >= HALF else neg_ref)[jy * HALF + i % HALF]

    def whole(ref):
        return lambda jy, i: ref[jy * NQ + i]

    before, after = jnp.maximum(slab - 1, 0), jnp.minimum(slab + 1, NS - 1)
    near, far = half_of(n1_ref, p1_ref), half_of(n2_ref, p2_ref)
    for here, halves, source, beside, sink in (
        (slab, (0, 1), whole(f_ref), near, f1_ref),
        (before, (1,), near, far, h1_ref),
        (after, (0,), near, far, h1_ref),
    ):
        advance([pred_ref[k, here] for k in range(8)], here, halves, source, beside, sink)
    advance(last, slab, (0, 1), whole(f1_ref), whole(h1_ref), out_ref)


def call(kernel, out, args, scratch=()):
    smem = pl.BlockSpec(memory_space=pltpu.SMEM)
    vmem = pl.BlockSpec(memory_space=pltpu.VMEM)
    return pl.pallas_call(
        kernel,
        out_shape=jax.ShapeDtypeStruct(out, F32),
        in_specs=[smem] + [vmem] * (len(args) - 1),
        out_specs=vmem,
        scratch_shapes=[pltpu.VMEM(s, F32) for s in scratch],
    )(*args)


def shifted(block, distance):
    count = NS
    return lax.ppermute(block, SLAB, [(i, i + distance) for i in range(count) if 0 <= i + distance < count])


def body(f_start, links, solid):
    rank, slab = lax.axis_index(VEL), lax.axis_index(SLAB)
    place = jnp.stack([rank, slab]).astype(jnp.int32)
    f = f_start.reshape(LY * NQ, NY, NZ)
    links = links.reshape(3, NY, NZ)
    solid = solid.reshape(NY, NZ)
    split = f.reshape(LY, 2, HALF, NY, NZ)
    falling = split[:, 0].reshape(LY * HALF, NY, NZ)
    rising = split[:, 1].reshape(LY * HALF, NY, NZ)
    p1, n1 = shifted(rising, 1), shifted(falling, -1)
    p2, n2 = shifted(rising, 2), shifted(falling, -2)

    parts = call(moments_kernel, (256, NZ), (place, f, links))
    parts = lax.all_to_all(parts.reshape(64, 4, NZ), VEL, 0, 0, tiled=True)
    owned = call(owner_kernel, (32, 8, NZ), (place, parts.reshape(32, 8, NZ), links, solid))
    owned = lax.all_to_all(owned, SLAB + ("zl",), 0, 0, tiled=True)
    block = call(combine_kernel, (16, 80, NZ), (place, owned.reshape(256, NZ)))
    got = lax.all_to_all(block, ("x", "y"), 0, 0, tiled=True)
    plane = (NY, NZ)
    out = call(
        finish_kernel,
        f.shape,
        (place, got.reshape(16, 10, 8, NZ), f, p1, p2, n1, n2),
        (
            (2, 8, NS) + plane,
            (4, NS + 2) + plane,
            (7, NS + 2) + plane,
            (8, NS) + plane,
            (8, NS + 4) + plane,
            (NQ,) + plane,
            (NQ,) + plane,
            f.shape,
            f.shape,
        ),
    )
    return out.reshape(f_start.shape)


def solution(mesh):
    fine = Mesh(mesh.devices.reshape(4, 2, 4, 4, 4), SLAB + VEL)
    in_specs = (P(VEL, SLAB, None, None), P(None, SLAB, None, None), P(SLAB, None, None))
    out_specs = P(VEL, SLAB, None, None)
    return jax.shard_map(body, mesh=fine, in_specs=in_specs, out_specs=out_specs, check_vma=False)
```

```python
import math

import jax
import jax.numpy as jnp
from jax import lax
from jax.experimental import pallas as pl
from jax.experimental.pallas import tpu as pltpu
from jax.sharding import Mesh
from jax.sharding import PartitionSpec as P


NQ = 16
HALF = NQ // 2
LY = 4
NS = 8
NY, NZ = 8, 128
SPACING = 0.6
COURANT = 0.06
RELAXATION_FREQ = 0.5
VISCOUS_TO_HEAT = 2.0 / 3.0
QUAD_WEIGHT = SPACING**3 / (2.0 * math.pi) ** 1.5
F32 = jnp.float32
LIMIT = 4 << 20

SLAB = ("zh", "core")
VEL = ("x", "y", "zl")


def rows_and_lanes():
    row = lax.broadcasted_iota(jnp.int32, (NY, NZ), 0)
    lane = lax.broadcasted_iota(jnp.int32, (NY, NZ), 1)
    return row, lane


def down(v, axis):
    return pltpu.roll(v, 1, axis)


def up(v, axis):
    return pltpu.roll(v, v.shape[axis] - 1, axis)


def speed_of(index):
    return (index.astype(F32) - (NQ - 1) / 2.0) * SPACING


def sides(links, axis, first, last, rising):
    open_up = links
    open_low = jnp.where(first, 0.0, down(links, axis))
    inner_up = jnp.where(last, 0.0, links)
    return jnp.where(rising, open_up, open_low), jnp.where(rising, open_low, inner_up)


def moments_kernel(f_ref, links_ref, out_ref, inner_ref, outer_ref):
    core = lax.axis_index("core")
    for jy in range(LY):
        inner_ref[pl.ds(jy * HALF, HALF)] = f_ref[pl.ds(jy * NQ + (1 - core) * HALF, HALF)]
        outer_ref[pl.ds(jy * HALF, HALF)] = f_ref[pl.ds(jy * NQ + core * HALF, HALF)]
    rank = lax.axis_index(VEL)
    row, lane = rows_and_lanes()
    zv = speed_of(rank // 4)
    z_rising, y_rising = rank // 4 >= HALF, rank % 4 >= 2
    ly = links_ref[1].astype(F32)
    lz = links_ref[2].astype(F32)
    out_y, in_y = sides(ly, 0, row == 0, row == NY - 1, y_rising)
    out_z, in_z = sides(lz, 1, lane == 0, lane == NZ - 1, z_rising)
    shift_y = jnp.where(y_rising, 1, NY - 1)
    shift_z = jnp.where(z_rising, 1, NZ - 1)
    az = COURANT * jnp.abs(zv)
    out_z, in_z = az * out_z, az * in_z
    totals = None
    for jy in range(LY):
        yv = speed_of(rank % 4 * LY + jy)
        ay = COURANT * jnp.abs(yv)
        pos, neg = [None] * 5, [None] * 5
        for j in range(HALF):
            a = (j + 0.5) * SPACING
            fp = f_ref[jy * NQ + HALF + j]
            fn = f_ref[jy * NQ + HALF - 1 - j]
            for n in range(5):
                wp = fp if n == 0 else fp * a**n
                wn = fn if n == 0 else fn * a**n
                pos[n] = wp if pos[n] is None else pos[n] + wp
                neg[n] = wn if neg[n] is None else neg[n] + wn
        full = [pos[n] + neg[n] if n % 2 == 0 else pos[n] - neg[n] for n in range(4)]
        keep = 1.0 - ay * out_y - out_z
        moved = [
            keep * v + (ay * in_y) * pltpu.roll(v, shift_y, 0) + in_z * pltpu.roll(v, shift_z, 1)
            for v in full
        ]
        plus = pos[1:5]
        minus = [neg[1], -neg[2], neg[3], -neg[4]]
        q = yv * yv + zv * zv
        parts = []
        for a0, a1, a2, a3 in (full, moved, plus, minus):
            e0 = 0.5 * (a2 + q * a0)
            e1 = 0.5 * (a3 + q * a1)
            parts.append([a0, a1, yv * a0, e0, e1, yv * e0])
        if totals is None:
            totals = parts
        else:
            totals = [[t + p for t, p in zip(ts, ps)] for ts, ps in zip(totals, parts)]
    for kind, (b0, b1, by, e0, e1, ey) in enumerate(totals):
        for k, v in enumerate((b0, b1, by, zv * b0, e0, e1, ey, zv * e0)):
            out_ref[pl.ds(k * 32 + kind, NY, stride=4), :] = v * QUAD_WEIGHT


def owner_kernel(parts_ref, links_ref, solid_ref, out_ref):
    rank = lax.axis_index(VEL)
    k, y = rank // 8, rank % 8
    total = parts_ref[0]
    for i in range(1, 32):
        total = total + parts_ref[i]
    total = total + pltpu.roll(total, 4, 0)
    row = lax.broadcasted_iota(jnp.int32, (8, NZ), 0)
    flags = [links_ref[a, pl.ds(y, 1), :].astype(F32) for a in range(3)]
    flags.append(solid_ref[pl.ds(y, 1), :].astype(F32))
    kind = k % 4
    own = jnp.where(kind == 0, flags[0], jnp.where(kind == 1, flags[1], jnp.where(kind == 2, flags[2], flags[3])))
    block = jnp.where(row < 4, total, jnp.where(row == 4, flags[0], jnp.where(row == 5, own, 0.0)))
    for i in range(32):
        out_ref[pl.ds(6 * i, 6), :] = block[:6]


def combine_kernel(parts_ref, out_ref):
    rank = lax.axis_index(VEL)
    kinds = [parts_ref[pl.ds(kind, 32, stride=6), :] for kind in range(6)]
    m0, q, hp, hm, lx, own = kinds
    row = lax.broadcasted_iota(jnp.int32, (32, NZ), 0)
    low = jnp.where(row < 4, 0.0, pltpu.roll(lx, 4, 0))
    inner = jnp.where(row >= 28, 0.0, lx)
    mt = q - COURANT * (lx * hp + low * hm - low * pltpu.roll(hp, 4, 0) - inner * pltpu.roll(hm, 28, 0))
    half = jnp.where(rank // 32 == 0, own[:16], own[16:])
    mt_near = jnp.where(lax.axis_index(SLAB) < NS // 2, mt[:24], mt[8:])
    for i in range(out_ref.shape[0]):
        out_ref[i, 0:32, :] = m0
        out_ref[i, 32:56, :] = mt_near
        out_ref[i, 56:72, :] = half


def macro_state(p):
    rho = p[0]
    inv = 1.0 / rho
    u = [p[1 + a] * inv for a in range(3)]
    energy = p[4]
    u2 = u[0] * u[0] + u[1] * u[1] + u[2] * u[2]
    temp = (2.0 * energy * inv - u2) / 3.0
    stress = rho * temp
    nu = RELAXATION_FREQ * rho * jnp.exp(0.28 * jnp.log(temp))
    scale = (1.0 - VISCOUS_TO_HEAT) / (5.0 * stress * temp)
    s = [(p[5 + a] - u[a] * (energy + stress)) * scale for a in range(3)]
    inv_t = 1.0 / temp
    height = rho * inv_t * lax.sqrt(inv_t)
    return u, u2, inv_t, nu, s, height


def xi(i):
    return (i - (NQ - 1) / 2.0) * SPACING


def target_moments(u, u2, inv_t, s, height):
    half_t = -0.5 * inv_t
    one_d = []
    for a in range(3):
        m = [None] * 7
        for i in range(NQ):
            c = xi(i) - u[a]
            t = jnp.exp(c * c * half_t)
            for n in range(7):
                m[n] = t if m[n] is None else m[n] + t
                if n < 6:
                    t = t * c
        one_d.append(m)
    x, y, z = one_d
    made = {}

    def once(key, build):
        if key not in made:
            made[key] = build()
        return made[key]

    def xy(i, j):
        return once(("xy", i, j), lambda: x[i] * y[j])

    def xy2(i, j):
        return once(("xy2", i, j), lambda: xy(i + 2, j) + xy(i, j + 2))

    def plain(i, j, k):
        return once(("plain", i, j, k), lambda: xy(i, j) * z[k])

    def squared(i, j, k):
        return once(("squared", i, j, k), lambda: xy2(i, j) * z[k] + xy(i, j) * z[k + 2])

    def tilted(i, j, k):
        return once(("tilted", i, j, k), lambda: squared(i, j, k) * inv_t - 5.0 * plain(i, j, k))

    def tilted2(i, j, k):
        def build():
            xy4 = once(("xy4", i, j), lambda: xy2(i + 2, j) + xy2(i, j + 2))
            fourth = xy4 * z[k] + 2.0 * (xy2(i, j) * z[k + 2]) + xy(i, j) * z[k + 4]
            return fourth * inv_t - 5.0 * squared(i, j, k)

        return once(("tilted2", i, j, k), build)

    def unit(*axes):
        return tuple(axes.count(a) for a in range(3))

    def mean(first, with_c, *axes):
        return first(*unit(*axes)) + sum(s[a] * with_c(*unit(*axes, a)) for a in range(3))

    n0 = mean(plain, tilted)
    n1 = [mean(plain, tilted, a) for a in range(3)]
    n2 = {(a, b): mean(plain, tilted, a, b) for a in range(3) for b in range(a, 3)}
    n3 = [mean(squared, tilted2, a) for a in range(3)]
    weight = QUAD_WEIGHT * height
    j_e = 0.5 * (n2[0, 0] + n2[1, 1] + n2[2, 2] + u2 * n0) + u[0] * n1[0] + u[1] * n1[1] + u[2] * n1[2]
    rows = [n0] + [n1[a] + u[a] * n0 for a in range(3)] + [j_e]
    for a in range(3):
        cross = sum(u[b] * n2[min(a, b), max(a, b)] for b in range(3))
        rows.append(0.5 * (n3[a] + u2 * n1[a]) + cross + u[a] * j_e)
    return [weight * r for r in rows]


def neighbours(v, w):
    return w[2] * up(v, 0) + w[3] * down(v, 0) + w[4] * up(v, 1) + w[5] * down(v, 1)


def finish_kernel(
    got_ref, f_ref, inner1_ref, inner2_ref, outer1_ref, outer2_ref, out_ref, m_ref, l_ref, w_ref, pred_ref, next_ref,
    xe_ref, xc_ref, f1_ref, h1_ref,
):
    rank, slab, core = lax.axis_index(VEL), lax.axis_index(SLAB), lax.axis_index("core")
    row, lane = rows_and_lanes()
    low_half = row < 4
    zero = jnp.zeros((NY, NZ), F32)

    for a in range(4):
        l_ref[a, 0] = zero
        l_ref[a, NS + 1] = zero

    @pl.loop(0, 8)
    def _(k):
        for t in range(9):
            t0, t1 = got_ref[2 * k, t], got_ref[2 * k + 1, t]
            first = jnp.where(low_half, t0, pltpu.roll(t1, 4, 0))
            second = jnp.where(low_half, pltpu.roll(t0, 4, 0), t1)
            if t < 7:
                m_ref[t // 4, k, 2 * (t % 4)] = first
                m_ref[t // 4, k, 2 * (t % 4) + 1] = second
            else:
                base = 1 + k // 4 * 4 + 2 * (t - 7)
                l_ref[k % 4, base] = first
                l_ref[k % 4, base + 1] = second

    for a in range(7):
        w_ref[a, 0] = zero
        w_ref[a, NS + 1] = zero
    for s in range(NS):
        lx, lx_low = l_ref[0, s + 1], l_ref[0, s]
        ly, lz = l_ref[1, s + 1], l_ref[2, s + 1]
        ly_low = jnp.where(row == 0, 0.0, down(ly, 0))
        lz_low = jnp.where(lane == 0, 0.0, down(lz, 1))
        share = 1.0 / (1.0 + (lx + ly + lz + lx_low + ly_low + lz_low))
        w_ref[0, s + 1] = share * lx if s < NS - 1 else zero
        w_ref[1, s + 1] = share * lx_low
        w_ref[2, s + 1] = jnp.where(row == NY - 1, 0.0, share * ly)
        w_ref[3, s + 1] = share * ly_low
        w_ref[4, s + 1] = jnp.where(lane == NZ - 1, 0.0, share * lz)
        w_ref[5, s + 1] = share * lz_low
        w_ref[6, s + 1] = share

    @pl.loop(0, 8)
    def _(k):
        start = [m_ref[0, k, s] for s in range(NS)]
        now = start
        for _ in range(2):
            new = []
            for s in range(NS):
                w = [w_ref[a, s + 1] for a in range(7)]
                v = w[6] * start[s] + neighbours(now[s], w)
                if s < NS - 1:
                    v = v + w[0] * now[s + 1]
                if s > 0:
                    v = v + w[1] * now[s - 1]
                new.append(v)
            now = new
        for s in range(NS):
            pred_ref[k, s] = now[s]

    for k in range(8):
        for i in (0, 1, NS + 2, NS + 3):
            next_ref[k, i] = zero

    shift = jnp.where(slab < NS // 2, 0, 2)

    @pl.loop(jnp.maximum(slab - 2, 0), jnp.minimum(slab + 3, NS))
    def _(w):
        u, u2, inv_t, nu, s, height = macro_state([pred_ref[k, w] for k in range(8)])
        goal = target_moments(u, u2, inv_t, s, height)
        body = l_ref[3, w + 1] > 0
        share = 1.0 / (1.0 + nu)
        for k in range(8):
            fresh = (m_ref[1, k, w - shift] + nu * goal[k]) * share
            next_ref[k, w + 2] = jnp.where(body, m_ref[0, k, w], fresh)

    last = []
    for k in range(8):
        around = [next_ref[k, slab + i] for i in range(5)]
        mids = []
        for i in range(3):
            w = [w_ref[a, slab + i] for a in range(7)]
            mids.append(
                w[6] * around[i + 1] + w[0] * around[i + 2] + w[1] * around[i] + neighbours(around[i + 1], w)
            )
        w = [w_ref[a, slab + 1] for a in range(7)]
        last.append(w[6] * around[2] + w[0] * mids[2] + w[1] * mids[0] + neighbours(mids[1], w))

    zv = speed_of(rank // 4)
    z_rising, y_rising = rank // 4 >= HALF, rank % 4 >= 2
    shift_y = jnp.where(y_rising, 1, NY - 1)
    shift_z = jnp.where(z_rising, 1, NZ - 1)
    az = COURANT * jnp.abs(zv)

    def advance(planes, here, halves, source, beside, sink):
        u, _, inv_t, nu, s, height = macro_state(planes)
        half_t = -0.5 * inv_t
        for i in range(NQ):
            if i // HALF in halves:
                c = xi(i) - u[0]
                c2 = c * c
                xe_ref[i] = jnp.exp(c2 * half_t)
                xc_ref[i] = c2 * inv_t
        share = 1.0 / (1.0 + nu)
        lx, lx_low = l_ref[0, here + 1], l_ref[0, here]
        lx_in = jnp.where(here < NS - 1, lx, 0.0)
        body = l_ref[3, here + 1] > 0
        out_y, in_y = sides(l_ref[1, here + 1], 0, row == 0, row == NY - 1, y_rising)
        out_z, in_z = sides(l_ref[2, here + 1], 1, lane == 0, lane == NZ - 1, z_rising)
        move = COURANT * share
        in_z = az * share * in_z
        cz = zv - u[2]
        out_x = (move * lx_low, move * lx)
        in_x = (move * lx_in, move * lx_low)

        @pl.loop(0, LY)
        def _(jy):
            yv = speed_of(rank % 4 * LY + jy)
            ay = COURANT * jnp.abs(yv)
            cy = yv - u[1]
            c2 = cy * cy + cz * cz
            top = nu * share * height * jnp.exp(c2 * half_t)
            tilt = cy * s[1] + cz * s[2] - u[0] * s[0]
            lift = c2 * inv_t - 5.0
            keep = share * (1.0 - ay * out_y - az * out_z)
            from_y = ay * share * in_y
            for i in range(NQ):
                side = i // HALF
                if side in halves:
                    f = source(jy, i)
                    a = abs(xi(i))
                    goal = top * xe_ref[i] * (1.0 + (xi(i) * s[0] + tilt) * (xc_ref[i] + lift))
                    fresh = f * (keep - a * out_x[side]) + (a * in_x[side]) * beside(jy, i)
                    fresh = fresh + from_y * pltpu.roll(f, shift_y, 0) + in_z * pltpu.roll(f, shift_z, 1)
                    sink[jy * NQ + i] = jnp.where(body, f, fresh + goal)

    def halo(inner_ref, outer_ref):
        def load(jy, i):
            j = jy * HALF + i % HALF
            on_chip = core == (0 if i < HALF else 1)
            return jnp.where(on_chip, inner_ref[j], outer_ref[j])

        return load

    def whole(ref):
        return lambda jy, i: ref[jy * NQ + i]

    before, after = jnp.maximum(slab - 1, 0), jnp.minimum(slab + 1, NS - 1)
    near, far = halo(inner1_ref, outer1_ref), halo(inner2_ref, outer2_ref)
    for here, halves, source, beside, sink in (
        (slab, (0, 1), whole(f_ref), near, f1_ref),
        (before, (1,), near, far, h1_ref),
        (after, (0,), near, far, h1_ref),
    ):
        advance([pred_ref[k, here] for k in range(8)], here, halves, source, beside, sink)
    advance(last, slab, (0, 1), whole(f1_ref), whole(h1_ref), out_ref)


def call(kernel, out, args, scratch=(), limit=None, keep=pltpu.VMEM):
    vmem = pl.BlockSpec(memory_space=pltpu.VMEM)
    return pl.pallas_call(
        kernel,
        out_shape=[keep(shape, F32) for shape in out],
        in_specs=[vmem] * len(args),
        out_specs=[vmem] * len(out),
        scratch_shapes=[pltpu.VMEM(s, F32) for s in scratch],
        compiler_params=pltpu.CompilerParams(vmem_limit_bytes=limit),
    )(*args)


def over_chip(block):
    return lax.ppermute(block, "core", [(0, 1), (1, 0)])


def to_next_chip(block):
    pairs = [(i, i + 1) for i in range(1, NS - 1, 2)]
    return lax.ppermute(block, SLAB, pairs + [(b, a) for a, b in pairs])


def steps(f_start, links, solid):
    f = f_start.reshape(LY * NQ, NY, NZ)
    links = links.reshape(3, NY, NZ)
    solid = solid.reshape(NY, NZ)
    half = (LY * HALF, NY, NZ)
    parts, to_inner, to_outer = call(moments_kernel, ((256, NZ), half, half), (f, links))
    outer1 = to_next_chip(to_outer)
    inner1 = over_chip(to_inner)
    parts = lax.all_to_all(parts.reshape(64, 4, NZ), VEL, 0, 0, tiled=True)
    (owned,) = call(owner_kernel, ((192, NZ),), (parts.reshape(32, 8, NZ), links, solid), limit=LIMIT)
    owned = lax.all_to_all(owned.reshape(32, 1, 6 * NZ), SLAB + ("zl",), 0, 0, tiled=True)
    outer2 = to_next_chip(inner1)
    inner2 = over_chip(outer1)
    (block,) = call(combine_kernel, ((16, 72, NZ),), (owned.reshape(192, NZ),), limit=LIMIT)
    got = lax.all_to_all(block, ("x", "y"), 0, 0, tiled=True)
    plane = (NY, NZ)
    (out,) = call(
        finish_kernel,
        (f.shape,),
        (got.reshape(16, 9, 8, NZ), f, inner1, inner2, outer1, outer2),
        (
            (2, 8, NS) + plane,
            (4, NS + 2) + plane,
            (7, NS + 2) + plane,
            (8, NS) + plane,
            (8, NS + 4) + plane,
            (NQ,) + plane,
            (NQ,) + plane,
            f.shape,
            f.shape,
        ),
        limit=16 << 20,
        keep=jax.ShapeDtypeStruct,
    )
    return out.reshape(f_start.shape)


def solution(mesh):
    fine = Mesh(mesh.devices.reshape(4, 2, 4, 4, 4), SLAB + VEL)
    in_specs = (P(VEL, SLAB, None, None), P(None, SLAB, None, None), P(SLAB, None, None))
    out_specs = P(VEL, SLAB, None, None)
    return jax.shard_map(steps, mesh=fine, in_specs=in_specs, out_specs=out_specs, check_vma=False)
```

```python
import math

import jax
import jax.numpy as jnp
from jax import lax
from jax.experimental import pallas as pl
from jax.experimental.pallas import tpu as pltpu
from jax.sharding import Mesh
from jax.sharding import PartitionSpec as P


NQ = 16
HALF = NQ // 2
LY = 4
NS = 8
NY, NZ = 8, 128
SPACING = 0.6
COURANT = 0.06
RELAXATION_FREQ = 0.5
VISCOUS_TO_HEAT = 2.0 / 3.0
QUAD_WEIGHT = SPACING**3 / (2.0 * math.pi) ** 1.5
F32 = jnp.float32
LIMIT = 4 << 20

SLAB = ("zh", "core")
VEL = ("x", "y", "zl")

MIDDLE = 42
VEL_ORDER = [MIDDLE] + list(range(1, MIDDLE)) + [0] + list(range(MIDDLE + 1, 64))
Z_ORDER = list(range(16, 32)) + list(range(16))
XY_FIRST = 10
XY_ORDER = list(range(XY_FIRST, 16)) + list(range(XY_FIRST))


def rows_and_lanes():
    row = lax.broadcasted_iota(jnp.int32, (NY, NZ), 0)
    lane = lax.broadcasted_iota(jnp.int32, (NY, NZ), 1)
    return row, lane


def down(v, axis):
    return pltpu.roll(v, 1, axis)


def up(v, axis):
    return pltpu.roll(v, v.shape[axis] - 1, axis)


def speed_of(index):
    return (index.astype(F32) - (NQ - 1) / 2.0) * SPACING


def sides(links, axis, first, last, rising):
    open_up = links
    open_low = jnp.where(first, 0.0, down(links, axis))
    inner_up = jnp.where(last, 0.0, links)
    return jnp.where(rising, open_up, open_low), jnp.where(rising, open_low, inner_up)


def moments_kernel(f_ref, links_ref, out_ref, inner_ref, outer_ref):
    core = lax.axis_index("core")
    for jy in range(LY):
        inner_ref[pl.ds(jy * HALF, HALF)] = f_ref[pl.ds(jy * NQ + (1 - core) * HALF, HALF)]
        outer_ref[pl.ds(jy * HALF, HALF)] = f_ref[pl.ds(jy * NQ + core * HALF, HALF)]
    rank = lax.axis_index(VEL)
    row, lane = rows_and_lanes()
    zv = speed_of(rank // 4)
    z_rising, y_rising = rank // 4 >= HALF, rank % 4 >= 2
    ly = links_ref[1].astype(F32)
    lz = links_ref[2].astype(F32)
    out_y, in_y = sides(ly, 0, row == 0, row == NY - 1, y_rising)
    out_z, in_z = sides(lz, 1, lane == 0, lane == NZ - 1, z_rising)
    shift_y = jnp.where(y_rising, 1, NY - 1)
    shift_z = jnp.where(z_rising, 1, NZ - 1)
    az = COURANT * jnp.abs(zv)
    out_z, in_z = az * out_z, az * in_z
    totals = None
    for jy in range(LY):
        yv = speed_of(rank % 4 * LY + jy)
        ay = COURANT * jnp.abs(yv)
        pos, neg = [None] * 5, [None] * 5
        for j in range(HALF):
            a = (j + 0.5) * SPACING
            fp = f_ref[jy * NQ + HALF + j]
            fn = f_ref[jy * NQ + HALF - 1 - j]
            for n in range(5):
                wp = fp if n == 0 else fp * a**n
                wn = fn if n == 0 else fn * a**n
                pos[n] = wp if pos[n] is None else pos[n] + wp
                neg[n] = wn if neg[n] is None else neg[n] + wn
        full = [pos[n] + neg[n] if n % 2 == 0 else pos[n] - neg[n] for n in range(4)]
        keep = 1.0 - ay * out_y - out_z
        moved = [
            keep * v + (ay * in_y) * pltpu.roll(v, shift_y, 0) + in_z * pltpu.roll(v, shift_z, 1)
            for v in full
        ]
        plus = pos[1:5]
        minus = [neg[1], -neg[2], neg[3], -neg[4]]
        q = yv * yv + zv * zv
        parts = []
        for a0, a1, a2, a3 in (full, moved, plus, minus):
            e0 = 0.5 * (a2 + q * a0)
            e1 = 0.5 * (a3 + q * a1)
            parts.append([a0, a1, yv * a0, e0, e1, yv * e0])
        if totals is None:
            totals = parts
        else:
            totals = [[t + p for t, p in zip(ts, ps)] for ts, ps in zip(totals, parts)]
    for kind, (b0, b1, by, e0, e1, ey) in enumerate(totals):
        for k, v in enumerate((b0, b1, by, zv * b0, e0, e1, ey, zv * e0)):
            out_ref[pl.ds(k * 32 + kind, NY, stride=4), :] = v * QUAD_WEIGHT
    first, middle = out_ref[pl.ds(0, 4), :], out_ref[pl.ds(4 * MIDDLE, 4), :]
    out_ref[pl.ds(0, 4), :] = middle
    out_ref[pl.ds(4 * MIDDLE, 4), :] = first


def owner_kernel(parts_ref, links_ref, solid_ref, out_ref):
    rank = lax.axis_index(VEL)
    k, y = rank // 8, rank % 8
    total = parts_ref[0]
    for i in range(1, 32):
        total = total + parts_ref[i]
    total = total + pltpu.roll(total, 4, 0)
    row = lax.broadcasted_iota(jnp.int32, (8, NZ), 0)
    flags = [links_ref[a, pl.ds(y, 1), :].astype(F32) for a in range(3)]
    flags.append(solid_ref[pl.ds(y, 1), :].astype(F32))
    kind = k % 4
    own = jnp.where(kind == 0, flags[0], jnp.where(kind == 1, flags[1], jnp.where(kind == 2, flags[2], flags[3])))
    block = jnp.where(row < 4, total, jnp.where(row == 4, flags[0], jnp.where(row == 5, own, 0.0)))
    for i in range(32):
        out_ref[pl.ds(6 * i, 6), :] = block[:6]


def combine_kernel(parts_ref, out_ref):
    rank = lax.axis_index(VEL)
    listed = [parts_ref[pl.ds(kind, 32, stride=6), :] for kind in range(6)]
    m0, q, hp, hm, lx, own = [jnp.concatenate([v[16:], v[:16]]) for v in listed]
    row = lax.broadcasted_iota(jnp.int32, (32, NZ), 0)
    low = jnp.where(row < 4, 0.0, pltpu.roll(lx, 4, 0))
    inner = jnp.where(row >= 28, 0.0, lx)
    mt = q - COURANT * (lx * hp + low * hm - low * pltpu.roll(hp, 4, 0) - inner * pltpu.roll(hm, 28, 0))
    half = jnp.where(rank // 32 == 0, own[:16], own[16:])
    mt_near = jnp.where(lax.axis_index(SLAB) < NS // 2, mt[:24], mt[8:])
    for i in range(out_ref.shape[0]):
        out_ref[i, 0:32, :] = m0
        out_ref[i, 32:56, :] = mt_near
        out_ref[i, 56:72, :] = half


def macro_state(p):
    rho = p[0]
    inv = 1.0 / rho
    u = [p[1 + a] * inv for a in range(3)]
    energy = p[4]
    u2 = u[0] * u[0] + u[1] * u[1] + u[2] * u[2]
    temp = (2.0 * energy * inv - u2) / 3.0
    stress = rho * temp
    nu = RELAXATION_FREQ * rho * jnp.exp(0.28 * jnp.log(temp))
    scale = (1.0 - VISCOUS_TO_HEAT) / (5.0 * stress * temp)
    s = [(p[5 + a] - u[a] * (energy + stress)) * scale for a in range(3)]
    inv_t = 1.0 / temp
    height = rho * inv_t * lax.sqrt(inv_t)
    return u, u2, inv_t, nu, s, height


def xi(i):
    return (i - (NQ - 1) / 2.0) * SPACING


def target_moments(u, u2, inv_t, s, height):
    half_t = -0.5 * inv_t
    one_d = []
    for a in range(3):
        m = [None] * 7
        for i in range(NQ):
            c = xi(i) - u[a]
            t = jnp.exp(c * c * half_t)
            for n in range(7):
                m[n] = t if m[n] is None else m[n] + t
                if n < 6:
                    t = t * c
        one_d.append(m)
    x, y, z = one_d
    made = {}

    def once(key, build):
        if key not in made:
            made[key] = build()
        return made[key]

    def xy(i, j):
        return once(("xy", i, j), lambda: x[i] * y[j])

    def xy2(i, j):
        return once(("xy2", i, j), lambda: xy(i + 2, j) + xy(i, j + 2))

    def plain(i, j, k):
        return once(("plain", i, j, k), lambda: xy(i, j) * z[k])

    def squared(i, j, k):
        return once(("squared", i, j, k), lambda: xy2(i, j) * z[k] + xy(i, j) * z[k + 2])

    def tilted(i, j, k):
        return once(("tilted", i, j, k), lambda: squared(i, j, k) * inv_t - 5.0 * plain(i, j, k))

    def tilted2(i, j, k):
        def build():
            xy4 = once(("xy4", i, j), lambda: xy2(i + 2, j) + xy2(i, j + 2))
            fourth = xy4 * z[k] + 2.0 * (xy2(i, j) * z[k + 2]) + xy(i, j) * z[k + 4]
            return fourth * inv_t - 5.0 * squared(i, j, k)

        return once(("tilted2", i, j, k), build)

    def unit(*axes):
        return tuple(axes.count(a) for a in range(3))

    def mean(first, with_c, *axes):
        return first(*unit(*axes)) + sum(s[a] * with_c(*unit(*axes, a)) for a in range(3))

    n0 = mean(plain, tilted)
    n1 = [mean(plain, tilted, a) for a in range(3)]
    n2 = {(a, b): mean(plain, tilted, a, b) for a in range(3) for b in range(a, 3)}
    n3 = [mean(squared, tilted2, a) for a in range(3)]
    weight = QUAD_WEIGHT * height
    j_e = 0.5 * (n2[0, 0] + n2[1, 1] + n2[2, 2] + u2 * n0) + u[0] * n1[0] + u[1] * n1[1] + u[2] * n1[2]
    rows = [n0] + [n1[a] + u[a] * n0 for a in range(3)] + [j_e]
    for a in range(3):
        cross = sum(u[b] * n2[min(a, b), max(a, b)] for b in range(3))
        rows.append(0.5 * (n3[a] + u2 * n1[a]) + cross + u[a] * j_e)
    return [weight * r for r in rows]


def neighbours(v, w):
    return w[2] * up(v, 0) + w[3] * down(v, 0) + w[4] * up(v, 1) + w[5] * down(v, 1)


def finish_kernel(
    got_ref, f_ref, inner1_ref, inner2_ref, outer1_ref, outer2_ref, out_ref, m_ref, l_ref, w_ref, pred_ref, next_ref,
    xe_ref, xc_ref, f1_ref, h1_ref,
):
    rank, slab, core = lax.axis_index(VEL), lax.axis_index(SLAB), lax.axis_index("core")
    row, lane = rows_and_lanes()
    low_half = row < 4
    zero = jnp.zeros((NY, NZ), F32)

    for a in range(4):
        l_ref[a, 0] = zero
        l_ref[a, NS + 1] = zero

    @pl.loop(0, 8)
    def _(k):
        at = lax.rem(2 * k + 16 - XY_FIRST, 16)
        for t in range(9):
            t0, t1 = got_ref[at, t], got_ref[at + 1, t]
            first = jnp.where(low_half, t0, pltpu.roll(t1, 4, 0))
            second = jnp.where(low_half, pltpu.roll(t0, 4, 0), t1)
            if t < 7:
                m_ref[t // 4, k, 2 * (t % 4)] = first
                m_ref[t // 4, k, 2 * (t % 4) + 1] = second
            else:
                base = 1 + k // 4 * 4 + 2 * (t - 7)
                l_ref[k % 4, base] = first
                l_ref[k % 4, base + 1] = second

    for a in range(7):
        w_ref[a, 0] = zero
        w_ref[a, NS + 1] = zero
    for s in range(NS):
        lx, lx_low = l_ref[0, s + 1], l_ref[0, s]
        ly, lz = l_ref[1, s + 1], l_ref[2, s + 1]
        ly_low = jnp.where(row == 0, 0.0, down(ly, 0))
        lz_low = jnp.where(lane == 0, 0.0, down(lz, 1))
        share = 1.0 / (1.0 + (lx + ly + lz + lx_low + ly_low + lz_low))
        w_ref[0, s + 1] = share * lx if s < NS - 1 else zero
        w_ref[1, s + 1] = share * lx_low
        w_ref[2, s + 1] = jnp.where(row == NY - 1, 0.0, share * ly)
        w_ref[3, s + 1] = share * ly_low
        w_ref[4, s + 1] = jnp.where(lane == NZ - 1, 0.0, share * lz)
        w_ref[5, s + 1] = share * lz_low
        w_ref[6, s + 1] = share

    @pl.loop(0, 8)
    def _(k):
        start = [m_ref[0, k, s] for s in range(NS)]
        now = start
        for _ in range(2):
            new = []
            for s in range(NS):
                w = [w_ref[a, s + 1] for a in range(7)]
                v = w[6] * start[s] + neighbours(now[s], w)
                if s < NS - 1:
                    v = v + w[0] * now[s + 1]
                if s > 0:
                    v = v + w[1] * now[s - 1]
                new.append(v)
            now = new
        for s in range(NS):
            pred_ref[k, s] = now[s]

    for k in range(8):
        for i in (0, 1, NS + 2, NS + 3):
            next_ref[k, i] = zero

    shift = jnp.where(slab < NS // 2, 0, 2)

    @pl.loop(jnp.maximum(slab - 2, 0), jnp.minimum(slab + 3, NS))
    def _(w):
        u, u2, inv_t, nu, s, height = macro_state([pred_ref[k, w] for k in range(8)])
        goal = target_moments(u, u2, inv_t, s, height)
        body = l_ref[3, w + 1] > 0
        share = 1.0 / (1.0 + nu)
        for k in range(8):
            fresh = (m_ref[1, k, w - shift] + nu * goal[k]) * share
            next_ref[k, w + 2] = jnp.where(body, m_ref[0, k, w], fresh)

    last = []
    for k in range(8):
        around = [next_ref[k, slab + i] for i in range(5)]
        mids = []
        for i in range(3):
            w = [w_ref[a, slab + i] for a in range(7)]
            mids.append(
                w[6] * around[i + 1] + w[0] * around[i + 2] + w[1] * around[i] + neighbours(around[i + 1], w)
            )
        w = [w_ref[a, slab + 1] for a in range(7)]
        last.append(w[6] * around[2] + w[0] * mids[2] + w[1] * mids[0] + neighbours(mids[1], w))

    zv = speed_of(rank // 4)
    z_rising, y_rising = rank // 4 >= HALF, rank % 4 >= 2
    shift_y = jnp.where(y_rising, 1, NY - 1)
    shift_z = jnp.where(z_rising, 1, NZ - 1)
    az = COURANT * jnp.abs(zv)

    def advance(planes, here, halves, source, beside, sink):
        u, _, inv_t, nu, s, height = macro_state(planes)
        half_t = -0.5 * inv_t
        for i in range(NQ):
            if i // HALF in halves:
                c = xi(i) - u[0]
                c2 = c * c
                xe_ref[i] = jnp.exp(c2 * half_t)
                xc_ref[i] = c2 * inv_t
        share = 1.0 / (1.0 + nu)
        lx, lx_low = l_ref[0, here + 1], l_ref[0, here]
        lx_in = jnp.where(here < NS - 1, lx, 0.0)
        body = l_ref[3, here + 1] > 0
        out_y, in_y = sides(l_ref[1, here + 1], 0, row == 0, row == NY - 1, y_rising)
        out_z, in_z = sides(l_ref[2, here + 1], 1, lane == 0, lane == NZ - 1, z_rising)
        move = COURANT * share
        in_z = az * share * in_z
        cz = zv - u[2]
        out_x = (move * lx_low, move * lx)
        in_x = (move * lx_in, move * lx_low)

        @pl.loop(0, LY)
        def _(jy):
            yv = speed_of(rank % 4 * LY + jy)
            ay = COURANT * jnp.abs(yv)
            cy = yv - u[1]
            c2 = cy * cy + cz * cz
            top = nu * share * height * jnp.exp(c2 * half_t)
            tilt = cy * s[1] + cz * s[2] - u[0] * s[0]
            lift = c2 * inv_t - 5.0
            keep = share * (1.0 - ay * out_y - az * out_z)
            from_y = ay * share * in_y
            for i in range(NQ):
                side = i // HALF
                if side in halves:
                    f = source(jy, i)
                    a = abs(xi(i))
                    goal = top * xe_ref[i] * (1.0 + (xi(i) * s[0] + tilt) * (xc_ref[i] + lift))
                    fresh = f * (keep - a * out_x[side]) + (a * in_x[side]) * beside(jy, i)
                    fresh = fresh + from_y * pltpu.roll(f, shift_y, 0) + in_z * pltpu.roll(f, shift_z, 1)
                    sink[jy * NQ + i] = jnp.where(body, f, fresh + goal)

    def halo(inner_ref, outer_ref):
        def load(jy, i):
            j = jy * HALF + i % HALF
            on_chip = core == (0 if i < HALF else 1)
            return jnp.where(on_chip, inner_ref[j], outer_ref[j])

        return load

    def whole(ref):
        return lambda jy, i: ref[jy * NQ + i]

    before, after = jnp.maximum(slab - 1, 0), jnp.minimum(slab + 1, NS - 1)
    near, far = halo(inner1_ref, outer1_ref), halo(inner2_ref, outer2_ref)
    for here, halves, source, beside, sink in (
        (slab, (0, 1), whole(f_ref), near, f1_ref),
        (before, (1,), near, far, h1_ref),
        (after, (0,), near, far, h1_ref),
    ):
        advance([pred_ref[k, here] for k in range(8)], here, halves, source, beside, sink)
    advance(last, slab, (0, 1), whole(f1_ref), whole(h1_ref), out_ref)


def call(kernel, out, args, scratch=(), limit=None, keep=pltpu.VMEM):
    vmem = pl.BlockSpec(memory_space=pltpu.VMEM)
    return pl.pallas_call(
        kernel,
        out_shape=[keep(shape, F32) for shape in out],
        in_specs=[vmem] * len(args),
        out_specs=[vmem] * len(out),
        scratch_shapes=[pltpu.VMEM(s, F32) for s in scratch],
        compiler_params=pltpu.CompilerParams(vmem_limit_bytes=limit),
    )(*args)


def over_chip(block):
    return lax.ppermute(block, "core", [(0, 1), (1, 0)])


def to_next_chip(block):
    pairs = [(i, i + 1) for i in range(1, NS - 1, 2)]
    return lax.ppermute(block, SLAB, pairs + [(b, a) for a, b in pairs])


def steps(f_start, links, solid):
    f = f_start.reshape(LY * NQ, NY, NZ)
    links = links.reshape(3, NY, NZ)
    solid = solid.reshape(NY, NZ)
    half = (LY * HALF, NY, NZ)
    parts, to_inner, to_outer = call(moments_kernel, ((256, NZ), half, half), (f, links))
    outer1 = to_next_chip(to_outer)
    inner1 = over_chip(to_inner)
    parts = lax.all_to_all(parts.reshape(64, 4, NZ), VEL, 0, 0, tiled=True, axis_index_groups=[VEL_ORDER])
    (owned,) = call(owner_kernel, ((192, NZ),), (parts.reshape(32, 8, NZ), links, solid), limit=LIMIT)
    owned = lax.all_to_all(owned.reshape(32, 1, 6 * NZ), SLAB + ("zl",), 0, 0, tiled=True, axis_index_groups=[Z_ORDER])
    outer2 = to_next_chip(inner1)
    inner2 = over_chip(outer1)
    (block,) = call(combine_kernel, ((16, 72, NZ),), (owned.reshape(192, NZ),), limit=LIMIT)
    got = lax.all_to_all(block, ("x", "y"), 0, 0, tiled=True, axis_index_groups=[XY_ORDER])
    plane = (NY, NZ)
    (out,) = call(
        finish_kernel,
        (f.shape,),
        (got.reshape(16, 9, 8, NZ), f, inner1, inner2, outer1, outer2),
        (
            (2, 8, NS) + plane,
            (4, NS + 2) + plane,
            (7, NS + 2) + plane,
            (8, NS) + plane,
            (8, NS + 4) + plane,
            (NQ,) + plane,
            (NQ,) + plane,
            f.shape,
            f.shape,
        ),
        limit=16 << 20,
        keep=jax.ShapeDtypeStruct,
    )
    return out.reshape(f_start.shape)


def solution(mesh):
    fine = Mesh(mesh.devices.reshape(4, 2, 4, 4, 4), SLAB + VEL)
    in_specs = (P(VEL, SLAB, None, None), P(None, SLAB, None, None), P(SLAB, None, None))
    out_specs = P(VEL, SLAB, None, None)
    return jax.shard_map(steps, mesh=fine, in_specs=in_specs, out_specs=out_specs, check_vma=False)
```

```python
import math

import jax
import jax.numpy as jnp
from jax import lax
from jax.experimental import pallas as pl
from jax.experimental.pallas import tpu as pltpu
from jax.sharding import Mesh
from jax.sharding import PartitionSpec as P


NQ = 16
HALF = NQ // 2
LY = 4
NS = 8
NY, NZ = 8, 128
SPACING = 0.6
COURANT = 0.06
RELAXATION_FREQ = 0.5
VISCOUS_TO_HEAT = 2.0 / 3.0
QUAD_WEIGHT = SPACING**3 / (2.0 * math.pi) ** 1.5
F32 = jnp.float32
LIMIT = 4 << 20

SLAB = ("zh", "core")
VEL = ("x", "y", "zl")

MIDDLE = 42
VEL_ORDER = [MIDDLE] + list(range(1, MIDDLE)) + [0] + list(range(MIDDLE + 1, 64))
Z_ORDER = list(range(16, 32)) + list(range(16))
XY_FIRST = 10
XY_ORDER = list(range(XY_FIRST, 16)) + list(range(XY_FIRST))


def rows_and_lanes():
    row = lax.broadcasted_iota(jnp.int32, (NY, NZ), 0)
    lane = lax.broadcasted_iota(jnp.int32, (NY, NZ), 1)
    return row, lane


def down(v, axis):
    return pltpu.roll(v, 1, axis)


def up(v, axis):
    return pltpu.roll(v, v.shape[axis] - 1, axis)


def speed_of(index):
    return (index.astype(F32) - (NQ - 1) / 2.0) * SPACING


def sides(links, axis, first, last, rising):
    open_up = links
    open_low = jnp.where(first, 0.0, down(links, axis))
    inner_up = jnp.where(last, 0.0, links)
    return jnp.where(rising, open_up, open_low), jnp.where(rising, open_low, inner_up)


def moments_kernel(f_ref, links_ref, out_ref, inner_ref, outer_ref):
    core = lax.axis_index("core")
    for jy in range(LY):
        inner_ref[pl.ds(jy * HALF, HALF)] = f_ref[pl.ds(jy * NQ + (1 - core) * HALF, HALF)]
        outer_ref[pl.ds(jy * HALF, HALF)] = f_ref[pl.ds(jy * NQ + core * HALF, HALF)]
    rank = lax.axis_index(VEL)
    row, lane = rows_and_lanes()
    zv = speed_of(rank // 4)
    z_rising, y_rising = rank // 4 >= HALF, rank % 4 >= 2
    ly = links_ref[1].astype(F32)
    lz = links_ref[2].astype(F32)
    out_y, in_y = sides(ly, 0, row == 0, row == NY - 1, y_rising)
    out_z, in_z = sides(lz, 1, lane == 0, lane == NZ - 1, z_rising)
    shift_y = jnp.where(y_rising, 1, NY - 1)
    shift_z = jnp.where(z_rising, 1, NZ - 1)
    az = COURANT * jnp.abs(zv)
    out_z, in_z = az * out_z, az * in_z
    totals = None
    for jy in range(LY):
        yv = speed_of(rank % 4 * LY + jy)
        ay = COURANT * jnp.abs(yv)
        pos, neg = [None] * 5, [None] * 5
        for j in range(HALF):
            a = (j + 0.5) * SPACING
            fp = f_ref[jy * NQ + HALF + j]
            fn = f_ref[jy * NQ + HALF - 1 - j]
            for n in range(5):
                wp = fp if n == 0 else fp * a**n
                wn = fn if n == 0 else fn * a**n
                pos[n] = wp if pos[n] is None else pos[n] + wp
                neg[n] = wn if neg[n] is None else neg[n] + wn
        full = [pos[n] + neg[n] if n % 2 == 0 else pos[n] - neg[n] for n in range(4)]
        keep = 1.0 - ay * out_y - out_z
        moved = [
            keep * v + (ay * in_y) * pltpu.roll(v, shift_y, 0) + in_z * pltpu.roll(v, shift_z, 1)
            for v in full
        ]
        plus = pos[1:5]
        minus = [neg[1], -neg[2], neg[3], -neg[4]]
        q = yv * yv + zv * zv
        parts = []
        for a0, a1, a2, a3 in (full, moved, plus, minus):
            e0 = 0.5 * (a2 + q * a0)
            e1 = 0.5 * (a3 + q * a1)
            parts.append([a0, a1, yv * a0, e0, e1, yv * e0])
        if totals is None:
            totals = parts
        else:
            totals = [[t + p for t, p in zip(ts, ps)] for ts, ps in zip(totals, parts)]
    for kind, (b0, b1, by, e0, e1, ey) in enumerate(totals):
        for k, v in enumerate((b0, b1, by, zv * b0, e0, e1, ey, zv * e0)):
            out_ref[pl.ds(k * 32 + kind, NY, stride=4), :] = v * QUAD_WEIGHT
    first, middle = out_ref[pl.ds(0, 4), :], out_ref[pl.ds(4 * MIDDLE, 4), :]
    out_ref[pl.ds(0, 4), :] = middle
    out_ref[pl.ds(4 * MIDDLE, 4), :] = first


def owner_kernel(parts_ref, links_ref, solid_ref, out_ref):
    rank = lax.axis_index(VEL)
    k, y = rank // 8, rank % 8
    total = parts_ref[0]
    for i in range(1, 32):
        total = total + parts_ref[i]
    total = total + pltpu.roll(total, 4, 0)
    row = lax.broadcasted_iota(jnp.int32, (8, NZ), 0)
    flags = [links_ref[a, pl.ds(y, 1), :].astype(F32) for a in range(3)]
    flags.append(solid_ref[pl.ds(y, 1), :].astype(F32))
    kind = k % 4
    own = jnp.where(kind == 0, flags[0], jnp.where(kind == 1, flags[1], jnp.where(kind == 2, flags[2], flags[3])))
    block = jnp.where(row < 4, total, jnp.where(row == 4, flags[0], jnp.where(row == 5, own, 0.0)))
    for i in range(32):
        out_ref[pl.ds(6 * i, 6), :] = block[:6]


def combine_kernel(parts_ref, out_ref):
    rank = lax.axis_index(VEL)
    listed = [parts_ref[pl.ds(kind, 32, stride=6), :] for kind in range(6)]
    m0, q, hp, hm, lx, own = [jnp.concatenate([v[16:], v[:16]]) for v in listed]
    row = lax.broadcasted_iota(jnp.int32, (32, NZ), 0)
    low = jnp.where(row < 4, 0.0, pltpu.roll(lx, 4, 0))
    inner = jnp.where(row >= 28, 0.0, lx)
    mt = q - COURANT * (lx * hp + low * hm - low * pltpu.roll(hp, 4, 0) - inner * pltpu.roll(hm, 28, 0))
    half = jnp.where(rank // 32 == 0, own[:16], own[16:])
    mt_near = jnp.where(lax.axis_index(SLAB) < NS // 2, mt[:24], mt[8:])
    for i in range(out_ref.shape[0]):
        out_ref[i, 0:32, :] = m0
        out_ref[i, 32:56, :] = mt_near
        out_ref[i, 56:72, :] = half


def macro_state(p):
    rho = p[0]
    inv = 1.0 / rho
    u = [p[1 + a] * inv for a in range(3)]
    energy = p[4]
    u2 = u[0] * u[0] + u[1] * u[1] + u[2] * u[2]
    temp = (2.0 * energy * inv - u2) / 3.0
    stress = rho * temp
    nu = RELAXATION_FREQ * rho * jnp.exp(0.28 * jnp.log(temp))
    scale = (1.0 - VISCOUS_TO_HEAT) / (5.0 * stress * temp)
    s = [(p[5 + a] - u[a] * (energy + stress)) * scale for a in range(3)]
    inv_t = 1.0 / temp
    height = rho * inv_t * lax.sqrt(inv_t)
    return u, u2, inv_t, nu, s, height


def xi(i):
    return (i - (NQ - 1) / 2.0) * SPACING


def target_moments(u, u2, inv_t, s, height):
    half_t = (-0.5 * math.log2(math.e)) * inv_t
    one_d = []
    for a in range(3):
        even, odd = [None] * 4, [None] * 3
        for j in range(HALF):
            d = (j + 0.5) * SPACING
            sides = []
            for c in (-d - u[a], d - u[a]):
                c2 = c * c
                levels = [jnp.exp2(c2 * half_t)]
                for _ in range(3):
                    levels.append(levels[-1] * c2)
                sides.append(levels)
            below, above = sides
            for n in range(4):
                t = below[n] + above[n]
                even[n] = t if even[n] is None else even[n] + t
            for n in range(3):
                t = d * (above[n] - below[n])
                odd[n] = t if odd[n] is None else odd[n] + t
        odd = [t - u[a] * e for t, e in zip(odd, even)]
        one_d.append([even[0], odd[0], even[1], odd[1], even[2], odd[2], even[3]])
    x, y, z = one_d
    made = {}

    def once(key, build):
        if key not in made:
            made[key] = build()
        return made[key]

    def xy(i, j):
        return once(("xy", i, j), lambda: x[i] * y[j])

    def xy2(i, j):
        return once(("xy2", i, j), lambda: xy(i + 2, j) + xy(i, j + 2))

    def plain(i, j, k):
        return once(("plain", i, j, k), lambda: xy(i, j) * z[k])

    def squared(i, j, k):
        return once(("squared", i, j, k), lambda: xy2(i, j) * z[k] + xy(i, j) * z[k + 2])

    def tilted(i, j, k):
        return once(("tilted", i, j, k), lambda: squared(i, j, k) * inv_t - 5.0 * plain(i, j, k))

    def tilted2(i, j, k):
        def build():
            xy4 = once(("xy4", i, j), lambda: xy2(i + 2, j) + xy2(i, j + 2))
            fourth = xy4 * z[k] + 2.0 * (xy2(i, j) * z[k + 2]) + xy(i, j) * z[k + 4]
            return fourth * inv_t - 5.0 * squared(i, j, k)

        return once(("tilted2", i, j, k), build)

    def unit(*axes):
        return tuple(axes.count(a) for a in range(3))

    def mean(first, with_c, *axes):
        return first(*unit(*axes)) + sum(s[a] * with_c(*unit(*axes, a)) for a in range(3))

    n0 = mean(plain, tilted)
    n1 = [mean(plain, tilted, a) for a in range(3)]
    n2 = {(a, b): mean(plain, tilted, a, b) for a in range(3) for b in range(a, 3)}
    n3 = [mean(squared, tilted2, a) for a in range(3)]
    weight = QUAD_WEIGHT * height
    j_e = 0.5 * (n2[0, 0] + n2[1, 1] + n2[2, 2] + u2 * n0) + u[0] * n1[0] + u[1] * n1[1] + u[2] * n1[2]
    rows = [n0] + [n1[a] + u[a] * n0 for a in range(3)] + [j_e]
    for a in range(3):
        cross = sum(u[b] * n2[min(a, b), max(a, b)] for b in range(3))
        rows.append(0.5 * (n3[a] + u2 * n1[a]) + cross + u[a] * j_e)
    return [weight * r for r in rows]


def neighbours(v, w):
    return w[2] * up(v, 0) + w[3] * down(v, 0) + w[4] * up(v, 1) + w[5] * down(v, 1)


def finish_kernel(
    got_ref, f_ref, inner1_ref, inner2_ref, outer1_ref, outer2_ref, out_ref, m_ref, l_ref, w_ref, pred_ref, next_ref,
    xe_ref, xc_ref, xs_ref, xo_ref, xn_ref, f1_ref, h1_ref,
):
    rank, slab, core = lax.axis_index(VEL), lax.axis_index(SLAB), lax.axis_index("core")
    row, lane = rows_and_lanes()
    low_half = row < 4
    zero = jnp.zeros((NY, NZ), F32)

    for a in range(4):
        l_ref[a, 0] = zero
        l_ref[a, NS + 1] = zero

    @pl.loop(0, 8)
    def _(k):
        at = lax.rem(2 * k + 16 - XY_FIRST, 16)
        for t in range(9):
            t0, t1 = got_ref[at, t], got_ref[at + 1, t]
            first = jnp.where(low_half, t0, pltpu.roll(t1, 4, 0))
            second = jnp.where(low_half, pltpu.roll(t0, 4, 0), t1)
            if t < 7:
                m_ref[t // 4, k, 2 * (t % 4)] = first
                m_ref[t // 4, k, 2 * (t % 4) + 1] = second
            else:
                base = 1 + k // 4 * 4 + 2 * (t - 7)
                l_ref[k % 4, base] = first
                l_ref[k % 4, base + 1] = second

    for a in range(7):
        w_ref[a, 0] = zero
        w_ref[a, NS + 1] = zero
    for s in range(NS):
        lx, lx_low = l_ref[0, s + 1], l_ref[0, s]
        ly, lz = l_ref[1, s + 1], l_ref[2, s + 1]
        ly_low = jnp.where(row == 0, 0.0, down(ly, 0))
        lz_low = jnp.where(lane == 0, 0.0, down(lz, 1))
        share = 1.0 / (1.0 + (lx + ly + lz + lx_low + ly_low + lz_low))
        w_ref[0, s + 1] = share * lx if s < NS - 1 else zero
        w_ref[1, s + 1] = share * lx_low
        w_ref[2, s + 1] = jnp.where(row == NY - 1, 0.0, share * ly)
        w_ref[3, s + 1] = share * ly_low
        w_ref[4, s + 1] = jnp.where(lane == NZ - 1, 0.0, share * lz)
        w_ref[5, s + 1] = share * lz_low
        w_ref[6, s + 1] = share

    @pl.loop(0, 8, unroll=2)
    def _(k):
        start = [m_ref[0, k, s] for s in range(NS)]
        now = start
        for _ in range(2):
            new = []
            for s in range(NS):
                w = [w_ref[a, s + 1] for a in range(7)]
                v = w[6] * start[s] + neighbours(now[s], w)
                if s < NS - 1:
                    v = v + w[0] * now[s + 1]
                if s > 0:
                    v = v + w[1] * now[s - 1]
                new.append(v)
            now = new
        for s in range(NS):
            pred_ref[k, s] = now[s]

    for k in range(8):
        for i in (0, 1, NS + 2, NS + 3):
            next_ref[k, i] = zero

    shift = jnp.where(slab < NS // 2, 0, 2)

    @pl.loop(jnp.maximum(slab - 2, 0), jnp.minimum(slab + 3, NS))
    def _(w):
        u, u2, inv_t, nu, s, height = macro_state([pred_ref[k, w] for k in range(8)])
        goal = target_moments(u, u2, inv_t, s, height)
        body = l_ref[3, w + 1] > 0
        share = 1.0 / (1.0 + nu)
        for k in range(8):
            fresh = (m_ref[1, k, w - shift] + nu * goal[k]) * share
            next_ref[k, w + 2] = jnp.where(body, m_ref[0, k, w], fresh)

    last = []
    for k in range(8):
        around = [next_ref[k, slab + i] for i in range(5)]
        mids = []
        for i in range(3):
            w = [w_ref[a, slab + i] for a in range(7)]
            mids.append(
                w[6] * around[i + 1] + w[0] * around[i + 2] + w[1] * around[i] + neighbours(around[i + 1], w)
            )
        w = [w_ref[a, slab + 1] for a in range(7)]
        last.append(w[6] * around[2] + w[0] * mids[2] + w[1] * mids[0] + neighbours(mids[1], w))

    zv = speed_of(rank // 4)
    z_rising, y_rising = rank // 4 >= HALF, rank % 4 >= 2
    shift_y = jnp.where(y_rising, 1, NY - 1)
    shift_z = jnp.where(z_rising, 1, NZ - 1)
    az = COURANT * jnp.abs(zv)

    def advance(planes, here, halves, source, beside, sink):
        u, _, inv_t, nu, s, height = macro_state(planes)
        half_t = -0.5 * inv_t
        share = 1.0 / (1.0 + nu)
        lx, lx_low = l_ref[0, here + 1], l_ref[0, here]
        lx_in = jnp.where(here < NS - 1, lx, 0.0)
        body = l_ref[3, here + 1] > 0
        out_y, in_y = sides(l_ref[1, here + 1], 0, row == 0, row == NY - 1, y_rising)
        out_z, in_z = sides(l_ref[2, here + 1], 1, lane == 0, lane == NZ - 1, z_rising)
        move = COURANT * share
        in_z = az * share * in_z
        cz = zv - u[2]
        out_x = (move * lx_low, move * lx)
        in_x = (move * lx_in, move * lx_low)
        for i in range(NQ):
            side = i // HALF
            if side in halves:
                c = xi(i) - u[0]
                c2 = c * c
                xe_ref[i] = jnp.exp(c2 * half_t)
                xc_ref[i] = c2 * inv_t
                xs_ref[i] = c * s[0]
                xo_ref[i] = abs(xi(i)) * out_x[side]
                xn_ref[i] = abs(xi(i)) * in_x[side]

        @pl.loop(0, LY, unroll=2 if len(halves) == 1 else 1)
        def _(jy):
            yv = speed_of(rank % 4 * LY + jy)
            ay = COURANT * jnp.abs(yv)
            cy = yv - u[1]
            c2 = cy * cy + cz * cz
            top = nu * share * height * jnp.exp(c2 * half_t)
            tilt = cy * s[1] + cz * s[2]
            lift = c2 * inv_t - 5.0
            keep = share * (1.0 - ay * out_y - az * out_z)
            from_y = ay * share * in_y
            for i in range(NQ):
                side = i // HALF
                if side in halves:
                    f = source(jy, i)
                    goal = top * xe_ref[i] * (1.0 + (xs_ref[i] + tilt) * (xc_ref[i] + lift))
                    fresh = f * (keep - xo_ref[i]) + xn_ref[i] * beside(jy, i)
                    fresh = fresh + from_y * pltpu.roll(f, shift_y, 0) + in_z * pltpu.roll(f, shift_z, 1)
                    sink[jy * NQ + i] = jnp.where(body, f, fresh + goal)

    def halo(inner_ref, outer_ref):
        def load(jy, i):
            j = jy * HALF + i % HALF
            on_chip = core == (0 if i < HALF else 1)
            return jnp.where(on_chip, inner_ref[j], outer_ref[j])

        return load

    def whole(ref):
        return lambda jy, i: ref[jy * NQ + i]

    before, after = jnp.maximum(slab - 1, 0), jnp.minimum(slab + 1, NS - 1)
    near, far = halo(inner1_ref, outer1_ref), halo(inner2_ref, outer2_ref)
    for here, halves, source, beside, sink in (
        (slab, (0, 1), whole(f_ref), near, f1_ref),
        (before, (1,), near, far, h1_ref),
        (after, (0,), near, far, h1_ref),
    ):
        advance([pred_ref[k, here] for k in range(8)], here, halves, source, beside, sink)
    advance(last, slab, (0, 1), whole(f1_ref), whole(h1_ref), out_ref)


def call(kernel, out, args, scratch=(), limit=None, keep=pltpu.VMEM):
    vmem = pl.BlockSpec(memory_space=pltpu.VMEM)
    return pl.pallas_call(
        kernel,
        out_shape=[keep(shape, F32) for shape in out],
        in_specs=[vmem] * len(args),
        out_specs=[vmem] * len(out),
        scratch_shapes=[pltpu.VMEM(s, F32) for s in scratch],
        compiler_params=pltpu.CompilerParams(vmem_limit_bytes=limit),
    )(*args)


def over_chip(block):
    return lax.ppermute(block, "core", [(0, 1), (1, 0)])


def to_next_chip(block):
    pairs = [(i, i + 1) for i in range(1, NS - 1, 2)]
    return lax.ppermute(block, SLAB, pairs + [(b, a) for a, b in pairs])


def steps(f_start, links, solid):
    f = f_start.reshape(LY * NQ, NY, NZ)
    links = links.reshape(3, NY, NZ)
    solid = solid.reshape(NY, NZ)
    half = (LY * HALF, NY, NZ)
    parts, to_inner, to_outer = call(moments_kernel, ((256, NZ), half, half), (f, links))
    outer1 = to_next_chip(to_outer)
    inner1 = over_chip(to_inner)
    parts = lax.all_to_all(parts.reshape(64, 4, NZ), VEL, 0, 0, tiled=True, axis_index_groups=[VEL_ORDER])
    (owned,) = call(owner_kernel, ((192, NZ),), (parts.reshape(32, 8, NZ), links, solid), limit=LIMIT)
    owned = lax.all_to_all(owned.reshape(32, 1, 6 * NZ), SLAB + ("zl",), 0, 0, tiled=True, axis_index_groups=[Z_ORDER])
    outer2 = to_next_chip(inner1)
    inner2 = over_chip(outer1)
    (block,) = call(combine_kernel, ((16, 72, NZ),), (owned.reshape(192, NZ),), limit=LIMIT)
    got = lax.all_to_all(block, ("x", "y"), 0, 0, tiled=True, axis_index_groups=[XY_ORDER])
    plane = (NY, NZ)
    (out,) = call(
        finish_kernel,
        (f.shape,),
        (got.reshape(16, 9, 8, NZ), f, inner1, inner2, outer1, outer2),
        (
            (2, 8, NS) + plane,
            (4, NS + 2) + plane,
            (7, NS + 2) + plane,
            (8, NS) + plane,
            (8, NS + 4) + plane,
            (NQ,) + plane,
            (NQ,) + plane,
            (NQ,) + plane,
            (NQ,) + plane,
            (NQ,) + plane,
            f.shape,
            f.shape,
        ),
        limit=16 << 20,
        keep=jax.ShapeDtypeStruct,
    )
    return out.reshape(f_start.shape)


def solution(mesh):
    fine = Mesh(mesh.devices.reshape(4, 2, 4, 4, 4), SLAB + VEL)
    in_specs = (P(VEL, SLAB, None, None), P(None, SLAB, None, None), P(SLAB, None, None))
    out_specs = P(VEL, SLAB, None, None)
    return jax.shard_map(steps, mesh=fine, in_specs=in_specs, out_specs=out_specs, check_vma=False)
```

```python
import math

import jax
import jax.numpy as jnp
from jax import lax
from jax.experimental import pallas as pl
from jax.experimental.pallas import tpu as pltpu
from jax.sharding import Mesh
from jax.sharding import PartitionSpec as P


NQ = 16
HALF = NQ // 2
LY = 4
NS = 8
NY, NZ = 8, 128
SPACING = 0.6
COURANT = 0.06
RELAXATION_FREQ = 0.5
VISCOUS_TO_HEAT = 2.0 / 3.0
QUAD_WEIGHT = SPACING**3 / (2.0 * math.pi) ** 1.5
F32 = jnp.float32
LIMIT = 4 << 20

SLAB = ("zh", "core")
VEL = ("x", "y", "zl")

MIDDLE = 42
VEL_ORDER = [MIDDLE] + list(range(1, MIDDLE)) + [0] + list(range(MIDDLE + 1, 64))
Z_ORDER = [16] + list(range(16)) + list(range(17, 32))
XY_FIRST = 10
XY_ORDER = [XY_FIRST] + list(range(XY_FIRST)) + list(range(XY_FIRST + 1, 16))


def rows_and_lanes():
    row = lax.broadcasted_iota(jnp.int32, (NY, NZ), 0)
    lane = lax.broadcasted_iota(jnp.int32, (NY, NZ), 1)
    return row, lane


def down(v, axis):
    return pltpu.roll(v, 1, axis)


def up(v, axis):
    return pltpu.roll(v, v.shape[axis] - 1, axis)


def speed_of(index):
    return (index.astype(F32) - (NQ - 1) / 2.0) * SPACING


def sides(links, axis, first, last, rising):
    open_up = links
    open_low = jnp.where(first, 0.0, down(links, axis))
    inner_up = jnp.where(last, 0.0, links)
    return jnp.where(rising, open_up, open_low), jnp.where(rising, open_low, inner_up)


def moments_kernel(f_ref, links_ref, out_ref, inner_ref, outer_ref):
    core = lax.axis_index("core")
    for jy in range(LY):
        inner_ref[pl.ds(jy * HALF, HALF)] = f_ref[pl.ds(jy * NQ + (1 - core) * HALF, HALF)]
        outer_ref[pl.ds(jy * HALF, HALF)] = f_ref[pl.ds(jy * NQ + core * HALF, HALF)]
    rank = lax.axis_index(VEL)
    row, lane = rows_and_lanes()
    zv = speed_of(rank // 4)
    z_rising, y_rising = rank // 4 >= HALF, rank % 4 >= 2
    ly = links_ref[1].astype(F32)
    lz = links_ref[2].astype(F32)
    out_y, in_y = sides(ly, 0, row == 0, row == NY - 1, y_rising)
    out_z, in_z = sides(lz, 1, lane == 0, lane == NZ - 1, z_rising)
    shift_y = jnp.where(y_rising, 1, NY - 1)
    shift_z = jnp.where(z_rising, 1, NZ - 1)
    az = COURANT * jnp.abs(zv)
    out_z, in_z = az * out_z, az * in_z
    totals = None
    for jy in range(LY):
        yv = speed_of(rank % 4 * LY + jy)
        ay = COURANT * jnp.abs(yv)
        pos, neg = [None] * 5, [None] * 5
        for j in range(HALF):
            a = (j + 0.5) * SPACING
            fp = f_ref[jy * NQ + HALF + j]
            fn = f_ref[jy * NQ + HALF - 1 - j]
            for n in range(5):
                wp = fp if n == 0 else fp * a**n
                wn = fn if n == 0 else fn * a**n
                pos[n] = wp if pos[n] is None else pos[n] + wp
                neg[n] = wn if neg[n] is None else neg[n] + wn
        full = [pos[n] + neg[n] if n % 2 == 0 else pos[n] - neg[n] for n in range(4)]
        keep = 1.0 - ay * out_y - out_z
        moved = [
            keep * v + (ay * in_y) * pltpu.roll(v, shift_y, 0) + in_z * pltpu.roll(v, shift_z, 1)
            for v in full
        ]
        plus = pos[1:5]
        minus = [neg[1], -neg[2], neg[3], -neg[4]]
        q = yv * yv + zv * zv
        parts = []
        for a0, a1, a2, a3 in (full, moved, plus, minus):
            e0 = 0.5 * (a2 + q * a0)
            e1 = 0.5 * (a3 + q * a1)
            parts.append([a0, a1, yv * a0, e0, e1, yv * e0])
        if totals is None:
            totals = parts
        else:
            totals = [[t + p for t, p in zip(ts, ps)] for ts, ps in zip(totals, parts)]
    for kind, (b0, b1, by, e0, e1, ey) in enumerate(totals):
        for k, v in enumerate((b0, b1, by, zv * b0, e0, e1, ey, zv * e0)):
            out_ref[pl.ds(k * 32 + kind, NY, stride=4), :] = v * QUAD_WEIGHT
    first, middle = out_ref[pl.ds(0, 4), :], out_ref[pl.ds(4 * MIDDLE, 4), :]
    out_ref[pl.ds(0, 4), :] = middle
    out_ref[pl.ds(4 * MIDDLE, 4), :] = first


def owner_kernel(parts_ref, links_ref, solid_ref, out_ref):
    rank = lax.axis_index(VEL)
    k, y = rank // 8, rank % 8
    total = parts_ref[0]
    for i in range(1, 32):
        total = total + parts_ref[i]
    total = total + pltpu.roll(total, 4, 0)
    row = lax.broadcasted_iota(jnp.int32, (8, NZ), 0)
    flags = [links_ref[a, pl.ds(y, 1), :].astype(F32) for a in range(3)]
    flags.append(solid_ref[pl.ds(y, 1), :].astype(F32))
    kind = k % 4
    own = jnp.where(kind == 0, flags[0], jnp.where(kind == 1, flags[1], jnp.where(kind == 2, flags[2], flags[3])))
    block = jnp.where(row < 4, total, jnp.where(row == 4, flags[0], jnp.where(row == 5, own, 0.0)))
    for i in range(32):
        out_ref[pl.ds(6 * i, 6), :] = block[:6]


def combine_kernel(parts_ref, out_ref):
    rank = lax.axis_index(VEL)
    listed = [parts_ref[pl.ds(kind, 32, stride=6), :] for kind in range(6)]
    row = lax.broadcasted_iota(jnp.int32, (32, NZ), 0)
    m0, q, hp, hm, lx, own = [
        jnp.where(row < 16, pltpu.roll(v, 31, 0), jnp.where(row == 16, pltpu.roll(v, 16, 0), v)) for v in listed
    ]
    low = jnp.where(row < 4, 0.0, pltpu.roll(lx, 4, 0))
    inner = jnp.where(row >= 28, 0.0, lx)
    mt = q - COURANT * (lx * hp + low * hm - low * pltpu.roll(hp, 4, 0) - inner * pltpu.roll(hm, 28, 0))
    half = jnp.where(rank // 32 == 0, own[:16], own[16:])
    mt_near = jnp.where(lax.axis_index(SLAB) < NS // 2, mt[:24], mt[8:])
    for i in range(out_ref.shape[0]):
        out_ref[i, 0:32, :] = m0
        out_ref[i, 32:56, :] = mt_near
        out_ref[i, 56:72, :] = half


def macro_state(p):
    rho = p[0]
    inv = 1.0 / rho
    u = [p[1 + a] * inv for a in range(3)]
    energy = p[4]
    u2 = u[0] * u[0] + u[1] * u[1] + u[2] * u[2]
    temp = (2.0 * energy * inv - u2) / 3.0
    stress = rho * temp
    nu = RELAXATION_FREQ * rho * jnp.exp(0.28 * jnp.log(temp))
    scale = (1.0 - VISCOUS_TO_HEAT) / (5.0 * stress * temp)
    s = [(p[5 + a] - u[a] * (energy + stress)) * scale for a in range(3)]
    inv_t = 1.0 / temp
    height = rho * inv_t * lax.sqrt(inv_t)
    return u, u2, inv_t, nu, s, height


def xi(i):
    return (i - (NQ - 1) / 2.0) * SPACING


def target_moments(u, u2, inv_t, s, height):
    half_t = (-0.5 * math.log2(math.e)) * inv_t
    one_d = []
    for a in range(3):
        even, odd = [None] * 4, [None] * 3
        for j in range(HALF):
            d = (j + 0.5) * SPACING
            sides = []
            for c in (-d - u[a], d - u[a]):
                c2 = c * c
                levels = [jnp.exp2(c2 * half_t)]
                for _ in range(3):
                    levels.append(levels[-1] * c2)
                sides.append(levels)
            below, above = sides
            for n in range(4):
                t = below[n] + above[n]
                even[n] = t if even[n] is None else even[n] + t
            for n in range(3):
                t = d * (above[n] - below[n])
                odd[n] = t if odd[n] is None else odd[n] + t
        odd = [t - u[a] * e for t, e in zip(odd, even)]
        one_d.append([even[0], odd[0], even[1], odd[1], even[2], odd[2], even[3]])
    x, y, z = one_d
    made = {}

    def once(key, build):
        if key not in made:
            made[key] = build()
        return made[key]

    def xy(i, j):
        return once(("xy", i, j), lambda: x[i] * y[j])

    def xy2(i, j):
        return once(("xy2", i, j), lambda: xy(i + 2, j) + xy(i, j + 2))

    def plain(i, j, k):
        return once(("plain", i, j, k), lambda: xy(i, j) * z[k])

    def squared(i, j, k):
        return once(("squared", i, j, k), lambda: xy2(i, j) * z[k] + xy(i, j) * z[k + 2])

    def tilted(i, j, k):
        return once(("tilted", i, j, k), lambda: squared(i, j, k) * inv_t - 5.0 * plain(i, j, k))

    def tilted2(i, j, k):
        def build():
            xy4 = once(("xy4", i, j), lambda: xy2(i + 2, j) + xy2(i, j + 2))
            fourth = xy4 * z[k] + 2.0 * (xy2(i, j) * z[k + 2]) + xy(i, j) * z[k + 4]
            return fourth * inv_t - 5.0 * squared(i, j, k)

        return once(("tilted2", i, j, k), build)

    def unit(*axes):
        return tuple(axes.count(a) for a in range(3))

    def mean(first, with_c, *axes):
        return first(*unit(*axes)) + sum(s[a] * with_c(*unit(*axes, a)) for a in range(3))

    n0 = mean(plain, tilted)
    n1 = [mean(plain, tilted, a) for a in range(3)]
    n2 = {(a, b): mean(plain, tilted, a, b) for a in range(3) for b in range(a, 3)}
    n3 = [mean(squared, tilted2, a) for a in range(3)]
    weight = QUAD_WEIGHT * height
    j_e = 0.5 * (n2[0, 0] + n2[1, 1] + n2[2, 2] + u2 * n0) + u[0] * n1[0] + u[1] * n1[1] + u[2] * n1[2]
    rows = [n0] + [n1[a] + u[a] * n0 for a in range(3)] + [j_e]
    for a in range(3):
        cross = sum(u[b] * n2[min(a, b), max(a, b)] for b in range(3))
        rows.append(0.5 * (n3[a] + u2 * n1[a]) + cross + u[a] * j_e)
    return [weight * r for r in rows]


def neighbours(v, w):
    return w[2] * up(v, 0) + w[3] * down(v, 0) + w[4] * up(v, 1) + w[5] * down(v, 1)


def finish_kernel(
    got_ref, f_ref, inner1_ref, inner2_ref, outer1_ref, outer2_ref, out_ref, m_ref, l_ref, w_ref, pred_ref, next_ref,
    xe_ref, xc_ref, xs_ref, xo_ref, xn_ref, f1_ref, h1_ref,
):
    rank, slab, core = lax.axis_index(VEL), lax.axis_index(SLAB), lax.axis_index("core")
    row, lane = rows_and_lanes()
    low_half = row < 4
    zero = jnp.zeros((NY, NZ), F32)

    for a in range(4):
        l_ref[a, 0] = zero
        l_ref[a, NS + 1] = zero

    @pl.loop(0, 8)
    def _(k):
        at = jnp.where(2 * k == XY_FIRST, 0, jnp.where(k < XY_FIRST // 2, 2 * k + 1, 2 * k))
        beside = jnp.where(k < XY_FIRST // 2, 2 * k + 2, 2 * k + 1)
        for t in range(9):
            t0, t1 = got_ref[at, t], got_ref[beside, t]
            first = jnp.where(low_half, t0, pltpu.roll(t1, 4, 0))
            second = jnp.where(low_half, pltpu.roll(t0, 4, 0), t1)
            if t < 7:
                m_ref[t // 4, k, 2 * (t % 4)] = first
                m_ref[t // 4, k, 2 * (t % 4) + 1] = second
            else:
                base = 1 + k // 4 * 4 + 2 * (t - 7)
                l_ref[k % 4, base] = first
                l_ref[k % 4, base + 1] = second

    for a in range(7):
        w_ref[a, 0] = zero
        w_ref[a, NS + 1] = zero
    for s in range(NS):
        lx, lx_low = l_ref[0, s + 1], l_ref[0, s]
        ly, lz = l_ref[1, s + 1], l_ref[2, s + 1]
        ly_low = jnp.where(row == 0, 0.0, down(ly, 0))
        lz_low = jnp.where(lane == 0, 0.0, down(lz, 1))
        share = 1.0 / (1.0 + (lx + ly + lz + lx_low + ly_low + lz_low))
        w_ref[0, s + 1] = share * lx if s < NS - 1 else zero
        w_ref[1, s + 1] = share * lx_low
        w_ref[2, s + 1] = jnp.where(row == NY - 1, 0.0, share * ly)
        w_ref[3, s + 1] = share * ly_low
        w_ref[4, s + 1] = jnp.where(lane == NZ - 1, 0.0, share * lz)
        w_ref[5, s + 1] = share * lz_low
        w_ref[6, s + 1] = share

    @pl.loop(0, 8, unroll=2)
    def _(k):
        start = [m_ref[0, k, s] for s in range(NS)]
        now = start
        for _ in range(2):
            new = []
            for s in range(NS):
                w = [w_ref[a, s + 1] for a in range(7)]
                v = w[6] * start[s] + neighbours(now[s], w)
                if s < NS - 1:
                    v = v + w[0] * now[s + 1]
                if s > 0:
                    v = v + w[1] * now[s - 1]
                new.append(v)
            now = new
        for s in range(NS):
            pred_ref[k, s] = now[s]

    for k in range(8):
        for i in (0, 1, NS + 2, NS + 3):
            next_ref[k, i] = zero

    shift = jnp.where(slab < NS // 2, 0, 2)

    @pl.loop(jnp.maximum(slab - 2, 0), jnp.minimum(slab + 3, NS))
    def _(w):
        u, u2, inv_t, nu, s, height = macro_state([pred_ref[k, w] for k in range(8)])
        goal = target_moments(u, u2, inv_t, s, height)
        body = l_ref[3, w + 1] > 0
        share = 1.0 / (1.0 + nu)
        for k in range(8):
            fresh = (m_ref[1, k, w - shift] + nu * goal[k]) * share
            next_ref[k, w + 2] = jnp.where(body, m_ref[0, k, w], fresh)

    last = []
    for k in range(8):
        around = [next_ref[k, slab + i] for i in range(5)]
        mids = []
        for i in range(3):
            w = [w_ref[a, slab + i] for a in range(7)]
            mids.append(
                w[6] * around[i + 1] + w[0] * around[i + 2] + w[1] * around[i] + neighbours(around[i + 1], w)
            )
        w = [w_ref[a, slab + 1] for a in range(7)]
        last.append(w[6] * around[2] + w[0] * mids[2] + w[1] * mids[0] + neighbours(mids[1], w))

    zv = speed_of(rank // 4)
    z_rising, y_rising = rank // 4 >= HALF, rank % 4 >= 2
    shift_y = jnp.where(y_rising, 1, NY - 1)
    shift_z = jnp.where(z_rising, 1, NZ - 1)
    az = COURANT * jnp.abs(zv)

    def advance(planes, here, halves, source, beside, sink):
        u, _, inv_t, nu, s, height = macro_state(planes)
        half_t = -0.5 * inv_t
        share = 1.0 / (1.0 + nu)
        lx, lx_low = l_ref[0, here + 1], l_ref[0, here]
        lx_in = jnp.where(here < NS - 1, lx, 0.0)
        body = l_ref[3, here + 1] > 0
        out_y, in_y = sides(l_ref[1, here + 1], 0, row == 0, row == NY - 1, y_rising)
        out_z, in_z = sides(l_ref[2, here + 1], 1, lane == 0, lane == NZ - 1, z_rising)
        move = COURANT * share
        in_z = az * share * in_z
        cz = zv - u[2]
        out_x = (move * lx_low, move * lx)
        in_x = (move * lx_in, move * lx_low)
        for i in range(NQ):
            side = i // HALF
            if side in halves:
                c = xi(i) - u[0]
                c2 = c * c
                xe_ref[i] = jnp.exp(c2 * half_t)
                xc_ref[i] = c2 * inv_t
                xs_ref[i] = c * s[0]
                xo_ref[i] = abs(xi(i)) * out_x[side]
                xn_ref[i] = abs(xi(i)) * in_x[side]

        @pl.loop(0, LY, unroll=2 if len(halves) == 1 else 1)
        def _(jy):
            yv = speed_of(rank % 4 * LY + jy)
            ay = COURANT * jnp.abs(yv)
            cy = yv - u[1]
            c2 = cy * cy + cz * cz
            top = nu * share * height * jnp.exp(c2 * half_t)
            tilt = cy * s[1] + cz * s[2]
            lift = c2 * inv_t - 5.0
            keep = share * (1.0 - ay * out_y - az * out_z)
            from_y = ay * share * in_y
            for i in range(NQ):
                side = i // HALF
                if side in halves:
                    f = source(jy, i)
                    goal = top * xe_ref[i] * (1.0 + (xs_ref[i] + tilt) * (xc_ref[i] + lift))
                    fresh = f * (keep - xo_ref[i]) + xn_ref[i] * beside(jy, i)
                    fresh = fresh + from_y * pltpu.roll(f, shift_y, 0) + in_z * pltpu.roll(f, shift_z, 1)
                    sink[jy * NQ + i] = jnp.where(body, f, fresh + goal)

    def halo(inner_ref, outer_ref):
        def load(jy, i):
            j = jy * HALF + i % HALF
            on_chip = core == (0 if i < HALF else 1)
            return jnp.where(on_chip, inner_ref[j], outer_ref[j])

        return load

    def whole(ref):
        return lambda jy, i: ref[jy * NQ + i]

    before, after = jnp.maximum(slab - 1, 0), jnp.minimum(slab + 1, NS - 1)
    near, far = halo(inner1_ref, outer1_ref), halo(inner2_ref, outer2_ref)
    for here, halves, source, beside, sink in (
        (slab, (0, 1), whole(f_ref), near, f1_ref),
        (before, (1,), near, far, h1_ref),
        (after, (0,), near, far, h1_ref),
    ):
        advance([pred_ref[k, here] for k in range(8)], here, halves, source, beside, sink)
    advance(last, slab, (0, 1), whole(f1_ref), whole(h1_ref), out_ref)


def call(kernel, out, args, scratch=(), limit=None, keep=pltpu.VMEM):
    vmem = pl.BlockSpec(memory_space=pltpu.VMEM)
    return pl.pallas_call(
        kernel,
        out_shape=[keep(shape, F32) for shape in out],
        in_specs=[vmem] * len(args),
        out_specs=[vmem] * len(out),
        scratch_shapes=[pltpu.VMEM(s, F32) for s in scratch],
        compiler_params=pltpu.CompilerParams(vmem_limit_bytes=limit),
    )(*args)


def over_chip(block):
    return lax.ppermute(block, "core", [(0, 1), (1, 0)])


def to_next_chip(block):
    pairs = [(i, i + 1) for i in range(1, NS - 1, 2)]
    return lax.ppermute(block, SLAB, pairs + [(b, a) for a, b in pairs])


def steps(f_start, links, solid):
    f = f_start.reshape(LY * NQ, NY, NZ)
    links = links.reshape(3, NY, NZ)
    solid = solid.reshape(NY, NZ)
    half = (LY * HALF, NY, NZ)
    parts, to_inner, to_outer = call(moments_kernel, ((256, NZ), half, half), (f, links))
    outer1 = to_next_chip(to_outer)
    inner1 = over_chip(to_inner)
    parts = lax.all_to_all(parts.reshape(64, 4, NZ), VEL, 0, 0, tiled=True, axis_index_groups=[VEL_ORDER])
    (owned,) = call(owner_kernel, ((192, NZ),), (parts.reshape(32, 8, NZ), links, solid), limit=LIMIT)
    owned = lax.all_to_all(owned.reshape(32, 1, 6 * NZ), SLAB + ("zl",), 0, 0, tiled=True, axis_index_groups=[Z_ORDER])
    outer2 = to_next_chip(inner1)
    inner2 = over_chip(outer1)
    (block,) = call(combine_kernel, ((16, 72, NZ),), (owned.reshape(192, NZ),), limit=LIMIT)
    got = lax.all_to_all(block, ("x", "y"), 0, 0, tiled=True, axis_index_groups=[XY_ORDER])
    plane = (NY, NZ)
    (out,) = call(
        finish_kernel,
        (f.shape,),
        (got.reshape(16, 9, 8, NZ), f, inner1, inner2, outer1, outer2),
        (
            (2, 8, NS) + plane,
            (4, NS + 2) + plane,
            (7, NS + 2) + plane,
            (8, NS) + plane,
            (8, NS + 4) + plane,
            (NQ,) + plane,
            (NQ,) + plane,
            (NQ,) + plane,
            (NQ,) + plane,
            (NQ,) + plane,
            f.shape,
            f.shape,
        ),
        limit=16 << 20,
        keep=jax.ShapeDtypeStruct,
    )
    return out.reshape(f_start.shape)


def solution(mesh):
    fine = Mesh(mesh.devices.reshape(4, 2, 4, 4, 4), SLAB + VEL)
    in_specs = (P(VEL, SLAB, None, None), P(None, SLAB, None, None), P(SLAB, None, None))
    out_specs = P(VEL, SLAB, None, None)
    return jax.shard_map(steps, mesh=fine, in_specs=in_specs, out_specs=out_specs, check_vma=False)
```
